32 devices in a mesh: rep: 2 (over x), bx: 16 (over z, y, core).
Axes of the slice: x: 2, y: 2, z: 4, core: 2. Of those that a mesh axis runs over, the one named last changes fastest.
Arguments:
- positions: float32 [128, 3, 128], P(('rep', 'bx')), parts along dimension 0, may hold values from 0 to 4.5
- species: int32 [128, 128], P(('rep', 'bx')), parts along dimension 0, may hold values from 0 to 88
- element_embed: bfloat16 [89, 128], replicated, may hold values from -6 to 6
- radial_one: float32 [8, 128], replicated, may hold values from -2 to 2
- mix_one: bfloat16 [128, 128], replicated, may hold values from -0.5 to 0.5
- radial_two: float32 [8, 128], replicated, may hold values from -2 to 2
- mix_two: bfloat16 [128, 128], replicated, may hold values from -0.5 to 0.5
- readout: bfloat16 [128], replicated, may hold values from -0.5 to 0.5
- tile_list: int32 [384, 2], P(('rep', 'bx')), parts along dimension 0, may hold values from 0 to 7, as said below
- tile_count: int32 [32], P(('rep', 'bx')), parts along dimension 0, may hold values from 4 to 12, as said below
- border: int32 [64, 2], P(('rep', 'bx')), parts along dimension 0, may hold values from 0 to 3, as said below
Outputs:
- atom_energy: float32 [128, 128], P(('rep', 'bx')), parts along dimension 0
- forces: float32 [128, 3, 128], P(('rep', 'bx')), parts along dimension 0
- descriptors: bfloat16 [128, 4, 128, 128], P(('rep', 'bx')), parts along dimension 0
The draws below stay inside these ranges and needn't reach their ends.
There are 2 independent parts, one for each index of `rep`. The reference program is written for one: setup_inputs(seed, part) draws one part's arguments, and reference() takes and returns one part's arrays. A program takes and returns all parts, laid end to end along the dimension named above; an argument that names none is the same for every part. Nothing has to cross between parts.
Inputs may be any that keep to these rules, and one draw needn't show every extreme that they name: `tile_list`: row 12 d + t belongs to slab d: its first entry is a cluster of that slab (0 to 3), its second a position in ext_d (0 to 7). `tile_count`: live tiles of a slab; 12 on at least one slab of every draw. `border`: rows 2 d and 2 d + 1 list distinct clusters of slab d, sent to its left and to its right neighbour.
All inputs are finite; a program needn't handle non-finite values.
Results may differ from the reference program's by a relative error of at most 0.0058.
Values may be sent and summed in bfloat16 or wider, within the bound.
No kernel may reach another device: no remote copies, remote signals or barrier semaphores. Data moves between devices by JAX's collectives and lax.ppermute only.
A program may use at most 64 MiB of HBM per device.

```python
import jax
import jax.numpy as jnp
from jax import lax

CHANNELS = 128
BASES = 8
ELEMENTS = 89
CLUSTER = 128
CL_DEV = 4
BORDER = 2
TILE_CAP = 12
CLUSTERS = 64
N_BX = 16


def draw_tile_list(key, part):
    key_center, key_partner = jax.random.split(jax.random.fold_in(key, 23))
    center = jax.random.randint(key_center, (N_BX * TILE_CAP, 1), 0, CL_DEV)
    partner = jax.random.randint(key_partner, (N_BX * TILE_CAP, 1), 0, CL_DEV + 2 * BORDER)
    return jnp.concatenate([center, partner], axis=1).astype(jnp.int32)


def draw_tile_count(key, part):
    key_heated, key_forced, key_normal = jax.random.split(jax.random.fold_in(key, 11), 3)
    forced = jax.random.randint(key_forced, (), 0, N_BX)
    heated = (jax.random.randint(key_heated, (N_BX,), 0, 8) == 0) | (jnp.arange(N_BX) == forced)
    normal_count = CL_DEV + jax.random.randint(key_normal, (N_BX,), 0, CL_DEV // 2 + 1)
    return jnp.where(heated, TILE_CAP, normal_count).astype(jnp.int32)


def draw_border(key, part):
    scores = jax.random.randint(jax.random.fold_in(key, 37), (2 * N_BX, CL_DEV), 0, 2 ** 20)
    ranking = scores * CL_DEV + jnp.arange(CL_DEV, dtype=jnp.int32)[None]
    ordering = jnp.argsort(ranking, axis=1, stable=True)
    return ordering[:, :BORDER].astype(jnp.int32)


def plant(result, own_key, smallest, top_value):
    shape = result.shape
    spot = [jax.random.randint(jax.random.fold_in(own_key, axis), (), 0, shape[axis]) for axis in range(len(shape))]
    result = result.at[tuple(spot)].set(smallest)
    longest = shape.index(max(shape))
    spot[longest] = (spot[longest] + 1) % shape[longest]
    return result.at[tuple(spot)].set(top_value)


def level_of(own_key, shape, cuts, low, largest):
    def one(axis_at, parts):
        steps = jax.random.uniform(jax.random.fold_in(jax.random.fold_in(own_key, 6), axis_at), (parts,), jnp.float32, low / len(cuts), largest / len(cuts))
        return jnp.repeat(jnp.exp(steps), shape[axis_at] // parts).reshape((-1,) + (1,) * (len(shape) - axis_at - 1))

    gain = one(*cuts[0])
    for cut in cuts[1:]:
        gain = gain * one(*cut)
    return gain


def noise(stream_key, shape, scale, bound, kind=jnp.bfloat16):
    return jnp.clip(scale * jax.random.normal(stream_key, shape, jnp.float32), -bound, bound).astype(kind)


def setup_inputs(seed: int = 0, part: int = 0) -> dict:
    splits = jax.random.split(jax.random.key(seed), 12)
    part_keys = jax.random.split(jax.random.fold_in(splits[11], part), 12)
    positions = jnp.clip(4.5 * jax.random.uniform(part_keys[0], (CLUSTERS, 3, CLUSTER), jnp.float32) ** level_of(part_keys[0], (CLUSTERS, 3, CLUSTER), ((0, 16),), -0.2, 0.2), 0.0, 4.5)
    species = plant(jax.random.randint(part_keys[1], (CLUSTERS, CLUSTER), 0, ELEMENTS), jax.random.fold_in(part_keys[1], 1), 0, ELEMENTS - 1).astype(jnp.int32)
    element_embed = noise(splits[2], (ELEMENTS, CHANNELS), 1.0, 6.0)
    radial_one = noise(splits[3], (BASES, CHANNELS), BASES ** -0.5, 2.0, jnp.float32)
    mix_one = noise(splits[4], (CHANNELS, CHANNELS), CHANNELS ** -0.5, 0.5)
    radial_two = noise(splits[5], (BASES, CHANNELS), BASES ** -0.5, 2.0, jnp.float32)
    mix_two = noise(splits[6], (CHANNELS, CHANNELS), CHANNELS ** -0.5, 0.5)
    readout = noise(splits[7], (CHANNELS,), CHANNELS ** -0.5, 0.5)
    tile_list = draw_tile_list(jax.random.fold_in(jax.random.fold_in(splits[11], part), 71), part)
    tile_count = draw_tile_count(jax.random.fold_in(jax.random.fold_in(splits[11], part), 71), part)
    border = draw_border(jax.random.fold_in(jax.random.fold_in(splits[11], part), 71), part)
    return {"positions": positions, "species": species, "element_embed": element_embed, "radial_one": radial_one, "mix_one": mix_one, "radial_two": radial_two, "mix_two": mix_two, "readout": readout, "tile_list": tile_list, "tile_count": tile_count, "border": border}


soften = 0.25
cutoff = 3.6
spread = 0.9
first_center = 0.25
center_step = 0.45
message_scale = 0.125
highest = lax.Precision.HIGHEST

def rounded(value):
    return lax.optimization_barrier(value.astype(jnp.bfloat16)).astype(jnp.float32)

def geometry(pos_center, pos_partner, same_cluster):
    offset = pos_partner[:, None, :] - pos_center[:, :, None]
    radius = jnp.sqrt(lax.optimization_barrier(jnp.sum(offset * offset, axis=0)) + soften)
    direction = offset / radius[None]
    cluster_size = radius.shape[0]
    centers = first_center + center_step * jnp.arange(BASES, dtype=jnp.float32)
    envelope = jnp.square(jnp.maximum(1.0 - jnp.square(radius / cutoff), 0.0))
    diagonal = (lax.broadcasted_iota(jnp.int32, (cluster_size, cluster_size), 0) == lax.broadcasted_iota(jnp.int32, (cluster_size, cluster_size), 1)).astype(jnp.float32)
    weight_mask = envelope * (1.0 - same_cluster * diagonal)
    radial_basis = jnp.exp(-jnp.square((radius[None] - centers[:, None, None]) / spread)) * weight_mask[None]
    harmonics = jnp.concatenate([jnp.ones_like(radius)[None], direction], axis=0)
    return radial_basis[:, :, None, :] * jnp.transpose(harmonics, (1, 0, 2))[None]

def extended_index(border):
    device = jnp.arange(N_BX, dtype=jnp.int32)
    left_device = (device - 1) % N_BX
    right_device = (device + 1) % N_BX
    from_left = left_device[:, None] * CL_DEV + border[2 * left_device + 1]
    own_index = device[:, None] * CL_DEV + jnp.arange(CL_DEV, dtype=jnp.int32)[None]
    from_right = right_device[:, None] * CL_DEV + border[2 * right_device]
    return jnp.concatenate([from_left, own_index, from_right], axis=1).astype(jnp.int32)

def tile_parts(rows_here, tile_index):
    center = rows_here[tile_index, 0]
    partner = rows_here[tile_index, 1]
    same_cluster = (partner == center + BORDER).astype(jnp.float32)
    return (center, partner, same_cluster)

def geometry_pullback(pos_here, center, partner, same_cluster, kernel_grad):

    def local_geometry(center_pos, partner_pos):
        return geometry(center_pos, partner_pos, same_cluster)
    pullback = jax.vjp(local_geometry, pos_here[center + BORDER], pos_here[partner])[1]
    return pullback(kernel_grad)

def reference(positions, species, element_embed, radial_one, mix_one, radial_two, mix_two, readout, tile_list, tile_count, border):
    index_ext = extended_index(border)
    flat_index = index_ext.reshape(-1)
    extent = CL_DEV + 2 * BORDER
    onehot = (species[..., None] == jnp.arange(ELEMENTS, dtype=jnp.int32)).astype(jnp.float32)
    own_feature = jnp.einsum('xas,sc->xac', onehot, element_embed.astype(jnp.float32), precision=highest)
    tile_rows = tile_list.reshape(N_BX, TILE_CAP, 2)
    live_mask = (jnp.arange(TILE_CAP, dtype=jnp.int32)[None] < tile_count[:, None]).astype(jnp.float32)
    tile_range = jnp.arange(TILE_CAP, dtype=jnp.int32)
    mix_one_wide = mix_one.astype(jnp.float32)
    mix_two_wide = mix_two.astype(jnp.float32)
    readout_wide = readout.astype(jnp.float32)
    pos_ext = positions[index_ext]
    feat_ext = own_feature[index_ext]

    def layer_one_device(inputs):
        pos_here, feat_here, rows_here, live_here = inputs

        def tile_step(totals, tile_index):
            center, partner, same_cluster = tile_parts(rows_here, tile_index)
            kernel = rounded(geometry(pos_here[center + BORDER], pos_here[partner], same_cluster))
            product = jnp.einsum('kamb,bc->kamc', kernel, feat_here[partner], precision=highest)
            message = message_scale * lax.optimization_barrier(jnp.sum(radial_one[:, None, None, :] * product, axis=0))
            return (totals.at[center].add(live_here[tile_index] * jnp.swapaxes(message, 0, 1)), None)
        start = jnp.zeros((CL_DEV, 4, CLUSTER, CHANNELS), jnp.float32)
        return lax.scan(tile_step, start, tile_range)[0]

    def layer_two_device(inputs):
        pos_here, feature_here, rows_here, live_here = inputs

        def tile_step(totals, tile_index):
            center, partner, same_cluster = tile_parts(rows_here, tile_index)
            kernel = rounded(geometry(pos_here[center + BORDER], pos_here[partner], same_cluster))
            product = jnp.einsum('kamb,mbc->kac', kernel, feature_here[partner], precision=highest)
            message = message_scale * lax.optimization_barrier(jnp.sum(radial_two[:, None, :] * product, axis=0))
            return (totals.at[center].add(live_here[tile_index] * message), None)
        start = jnp.zeros((CL_DEV, CLUSTER, CHANNELS), jnp.float32)
        return lax.scan(tile_step, start, tile_range)[0]

    def layer_two_back_device(inputs):
        pos_here, feature_here, rows_here, live_here, adjoint_here = inputs

        def tile_step(carry, tile_index):
            feature_grad, position_grad = carry
            center, partner, same_cluster = tile_parts(rows_here, tile_index)
            live_flag = live_here[tile_index]
            kernel = rounded(geometry(pos_here[center + BORDER], pos_here[partner], same_cluster))
            weighted = rounded(message_scale * radial_two[:, None, :] * adjoint_here[center][None])
            partner_grad = jnp.einsum('kamb,kac->mbc', kernel, weighted, precision=highest)
            kernel_grad = jnp.einsum('kac,mbc->kamb', weighted, feature_here[partner], precision=highest)
            grad_center, grad_partner = geometry_pullback(pos_here, center, partner, same_cluster, live_flag * kernel_grad)
            feature_grad = feature_grad.at[partner].add(live_flag * partner_grad)
            position_grad = position_grad.at[center + BORDER].add(grad_center).at[partner].add(grad_partner)
            return ((feature_grad, position_grad), None)
        start = (jnp.zeros((extent, 4, CLUSTER, CHANNELS), jnp.float32), jnp.zeros((extent, 3, CLUSTER), jnp.float32))
        return lax.scan(tile_step, start, tile_range)[0]

    def layer_one_back_device(inputs):
        pos_here, feat_here, rows_here, live_here, adjoint_here = inputs

        def tile_step(position_grad, tile_index):
            center, partner, same_cluster = tile_parts(rows_here, tile_index)
            live_flag = live_here[tile_index]
            weighted = rounded(message_scale * radial_one[:, None, None, :] * jnp.swapaxes(adjoint_here[center], 0, 1)[None])
            kernel_grad = jnp.einsum('kamc,bc->kamb', weighted, feat_here[partner], precision=highest)
            grad_center, grad_partner = geometry_pullback(pos_here, center, partner, same_cluster, live_flag * kernel_grad)
            return (position_grad.at[center + BORDER].add(grad_center).at[partner].add(grad_partner), None)
        start = jnp.zeros((extent, 3, CLUSTER), jnp.float32)
        return lax.scan(tile_step, start, tile_range)[0]
    first_sum = lax.map(layer_one_device, (pos_ext, feat_ext, tile_rows, live_mask))
    first_sum = first_sum.reshape(CLUSTERS, 4, CLUSTER, CHANNELS)
    mixed_one = jnp.einsum('xmac,cd->xmad', rounded(first_sum), mix_one_wide, precision=highest)
    mixed_one = mixed_one.at[:, 0].add(own_feature)
    layer_feature = rounded(mixed_one)
    feature_ext = layer_feature[index_ext]
    second_sum = lax.map(layer_two_device, (pos_ext, feature_ext, tile_rows, live_mask))
    second_sum = second_sum.reshape(CLUSTERS, CLUSTER, CHANNELS)
    activation = jnp.einsum('xac,cd->xad', rounded(second_sum), mix_two_wide, precision=highest)
    activation = activation + layer_feature[:, 0] + lax.optimization_barrier(jnp.sum(jnp.square(layer_feature[:, 1:]), axis=1))
    sigmoid_z = jax.nn.sigmoid(activation)
    atom_energy = lax.optimization_barrier(jnp.sum(activation * sigmoid_z * readout_wide, axis=-1))
    energy_adjoint = readout_wide * sigmoid_z * (1.0 + activation * (1.0 - sigmoid_z))
    second_adjoint = jnp.einsum('xae,ce->xac', energy_adjoint, mix_two_wide, precision=highest)
    direct_adjoint = jnp.concatenate([energy_adjoint[:, None], 2.0 * layer_feature[:, 1:] * energy_adjoint[:, None]], axis=1)
    adjoint_blocks = second_adjoint.reshape(N_BX, CL_DEV, CLUSTER, CHANNELS)
    feature_back, moves_two = lax.map(layer_two_back_device, (pos_ext, feature_ext, tile_rows, live_mask, adjoint_blocks))
    feature_adjoint = direct_adjoint.at[flat_index].add(feature_back.reshape(-1, 4, CLUSTER, CHANNELS))
    moves_total = jnp.zeros_like(positions).at[flat_index].add(moves_two.reshape(-1, 3, CLUSTER))
    first_adjoint = jnp.einsum('xmae,ce->xmac', feature_adjoint, mix_one_wide, precision=highest)
    first_blocks = first_adjoint.reshape(N_BX, CL_DEV, 4, CLUSTER, CHANNELS)
    moves_one = lax.map(layer_one_back_device, (pos_ext, feat_ext, tile_rows, live_mask, first_blocks))
    moves_total = moves_total.at[flat_index].add(moves_one.reshape(-1, 3, CLUSTER))
    return (atom_energy, -moves_total, layer_feature.astype(jnp.bfloat16))
```

```python
import math

import jax
import jax.numpy as jnp
from jax import lax
from jax.experimental import pallas as pl
from jax.experimental.pallas import tpu as pltpu
from jax.sharding import PartitionSpec as P

soften = 0.25
cutoff = 3.6
spread = 0.9
first_center = 0.25
center_step = 0.45
message_scale = 0.125
dead_shift = 60.0
f32 = jnp.float32
bf16 = jnp.bfloat16
STEP = 32
FINE = 16
ROWS = 8

contract_cols = (((1,), (1,)), ((), ()))
contract_rows = (((0,), (0,)), ((), ()))


def dot(left, right, dims=(((1,), (0,)), ((), ()))):
    return lax.dot_general(left, right, dims, preferred_element_type=f32)


def split(value):
    high = value.astype(bf16)
    return high, (value - high.astype(f32)).astype(bf16)


def wide_columns(pack, out_ref, at):
    size = pack.shape[-1]
    for e in range(3):
        out_ref[at, e] = jnp.transpose(jnp.broadcast_to(pack[e : e + 1, :], (size, size)))


def wide_radial(radial, out_ref):
    bases, channels = radial.shape
    for k in range(bases):
        out_ref[k] = jnp.transpose(
            jnp.broadcast_to(radial[k : k + 1, :] * message_scale, (channels, channels))
        )


def pair_geometry(cols, rows, partner_rows, shift, key, start):
    if partner_rows:
        offset = [col - row for row, col in zip(rows, cols)]
    else:
        offset = [row - col for row, col in zip(rows, cols)]
    square = offset[0] * offset[0] + offset[1] * offset[1] + (offset[2] * offset[2] + shift)
    inverse = lax.rsqrt(square)
    shifted = square * inverse - first_center
    fall = jnp.maximum(1.0 - square * (1.0 / (cutoff * cutoff)), 0.0)
    shape = cols[0].shape
    apart = lax.broadcasted_iota(jnp.int32, shape, 1) - lax.broadcasted_iota(jnp.int32, shape, 0)
    fall_masked = jnp.where(apart == key + start, 0.0, fall)
    scale = math.log2(math.e) / (spread * spread)
    gauss = jnp.exp2(shifted * shifted * -scale)
    ratio = jnp.exp2(shifted * (2.0 * center_step * scale))
    return offset, inverse, shifted, fall, fall_masked, gauss, ratio


def steps_of(bases):
    base = (center_step / spread) ** 2
    return [math.exp(-base * (2 * k - 1)) for k in range(1, bases)]


def select(tiles, count, order, keep):
    number = jnp.int32(0)
    for t in range(tiles.shape[1]):
        order[number] = t
        wanted = jnp.logical_and(t < count[0], keep(tiles[1, t]))
        number = number + wanted.astype(jnp.int32)
    return number


def tile_of(tiles, order, number, i, margin):
    t = order[jnp.maximum(jnp.minimum(i, number - 1), 0)]
    g, h = tiles[0, t], tiles[1, t]
    key = jnp.where(h == g + margin, 0, 1 << 20).astype(jnp.int32)
    shift = jnp.where(i < number, soften, soften + dead_shift).astype(f32)
    return g, h, shift, key


def pipelined(number, first, second):
    @pl.when(number > 0)
    def _():
        first(0, 0)

        def step(i, carry):
            second(2 * i, 0)
            first(2 * i + 1, 1)
            second(2 * i + 1, 1)
            first(2 * i + 2, 0)
            return carry

        lax.fori_loop(0, (number + 1) // 2, step, 0)


def write_kernel(writers, wide, row, partner_rows, shift, key, bases):
    size = row.shape[-1]
    ratios = steps_of(bases)
    rows = [row[e : e + 1, :] for e in range(3)]
    for start in range(0, size, STEP):
        cols = [wide(e, start, STEP) for e in range(3)]
        offset, inverse, _, fall, fall_masked, gauss, ratio = pair_geometry(
            cols, rows, partner_rows, shift, key, start
        )
        unit = [part * inverse for part in offset]
        basis = gauss * fall * fall_masked
        for k in range(bases):
            if k:
                basis = basis * (ratio * ratios[k - 1])
            for m in range(4):
                value = (basis if m == 0 else basis * unit[m - 1]).astype(bf16)
                for write in writers:
                    write(k, slice(m * size + start, m * size + start + STEP), value)


def writer(ref, *lead):
    def write(k, rows, value):
        ref[(*lead, k, rows)] = value

    return write


def reader(ref, at):
    return lambda e, start, step: ref[at, e, start : start + step, :]


def pack_kernel(border, positions, species, own_out, left_out, right_out):
    clusters, size = species.shape
    for g in range(clusters):
        own_out[g] = jnp.zeros((ROWS, size), f32)
        for e in range(3):
            own_out[g, e : e + 1, :] = positions[e, g : g + 1, :]
        own_out[g, 3:4, :] = species[g : g + 1, :].astype(f32)
    for s in range(border.shape[1]):
        left_out[s] = own_out[border[0, s]]
        right_out[s] = own_out[border[1, s]]


def embed_cluster(pack, embed, radial, embedded_out, weighted, rest, at, out_at):
    size = pack.shape[-1]
    col = jnp.transpose(pack)
    onehot = (
        lax.broadcasted_iota(jnp.int32, (size, embed.shape[0]), 1).astype(f32) == col[:, 3:4]
    ).astype(bf16)
    wide = dot(onehot, embed[...])
    embedded_out[out_at] = wide.astype(bf16)
    for k in range(radial.shape[0]):
        high, low = split(wide * (message_scale * radial[k : k + 1, :]))
        weighted[at, k * size : (k + 1) * size, :] = high
        rest[at, k * size : (k + 1) * size, :] = low


def layer_one_tiles(
    tiles, order, number, margin, wide_own, row_of, weights_of, kernels, total, bases
):
    def make(i, slot):
        g, h, shift, key = tile_of(tiles, order, number, i, margin)
        write_kernel(
            [writer(kernels[slot])], reader(wide_own, g), row_of(h), False, shift, key, bases
        )

    def use(i, slot):
        g, h, _, _ = tile_of(tiles, order, number, i, margin)
        both = dot(
            jnp.concatenate([kernels[slot][k] for k in range(bases)], axis=1),
            jnp.concatenate(weights_of(h), axis=1),
        )
        half = both.shape[1] // 2
        total[g] += both[:, :half] + both[:, half:]

    pipelined(number, make, use)


def one_own_kernel(
    tiles, count, own, embed, radial,
    embedded_out, wide_own, total,
    weighted, rest, kernel_a, kernel_b, order, *, margin,
):
    clusters = own.shape[0]
    bases = radial.shape[0]
    for g in range(clusters):
        wide_columns(own[g], wide_own, g)
        embed_cluster(own[g], embed, radial, embedded_out, weighted, rest, g, g)
    total[...] = jnp.zeros_like(total)
    number = select(
        tiles, count, order,
        lambda h: jnp.logical_and(h >= margin, h < margin + clusters),
    )
    layer_one_tiles(
        tiles, order, number, margin, wide_own,
        lambda h: own[jnp.clip(h - margin, 0, clusters - 1)],
        lambda h: [ref[jnp.clip(h - margin, 0, clusters - 1)] for ref in (weighted, rest)],
        (kernel_a, kernel_b), total, bases,
    )


def halo_slot(h, margin, clusters):
    return jnp.where(h < margin, h, jnp.maximum(h - clusters, 0))


def one_halo_kernel(
    tiles, count, border, left, right, own, embed, radial, mix, embedded_own, wide_own, total_own,
    feature_out, send_left, send_right, pack_out, embedded_out,
    weighted, rest, halo, kernel_a, kernel_b, total, order,
):
    clusters, _, size = own.shape
    margin = left.shape[0]
    bases = radial.shape[0]
    for s in range(margin):
        for at, ref, out_at in ((s, left, s), (margin + s, right, margin + clusters + s)):
            pack = ref[s]
            halo[at] = pack
            pack_out[out_at] = pack
            embed_cluster(pack, embed, radial, embedded_out, weighted, rest, at, out_at)
    for g in range(clusters):
        pack_out[margin + g] = own[g]
        embedded_out[margin + g] = embedded_own[g]
    total[...] = jnp.zeros_like(total)
    number = select(
        tiles, count, order,
        lambda h: jnp.logical_or(h < margin, h >= margin + clusters),
    )
    layer_one_tiles(
        tiles, order, number, margin, wide_own,
        lambda h: halo[halo_slot(h, margin, clusters)],
        lambda h: [ref[halo_slot(h, margin, clusters)] for ref in (weighted, rest)],
        (kernel_a, kernel_b), total, bases,
    )
    for g in range(clusters):
        mixed = dot((total[g] + total_own[g]).astype(bf16), mix[...])
        for m in range(4):
            part = mixed[m * size : (m + 1) * size]
            if m == 0:
                part = part + embedded_own[g].astype(f32)
            feature_out[g, m * size : (m + 1) * size, :] = part.astype(bf16)
    for s in range(margin):
        send_left[s] = feature_out[border[0, s]]
        send_right[s] = feature_out[border[1, s]]


def layer_two_tiles(
    tiles, order, number, margin, wide_ext, pack, feature_of, radial_wide, kernels, kept, total
):
    bases = radial_wide.shape[0]
    size = pack.shape[-1]

    def make(i, slot):
        g, h, shift, key = tile_of(tiles, order, number, i, margin)
        writers = [writer(kernels[slot])]
        if kept is not None:
            writers.append(writer(kept, i))
        write_kernel(writers, reader(wide_ext, h), pack[g + margin], True, shift, key, bases)

    def use(i, slot):
        g, h, _, _ = tile_of(tiles, order, number, i, margin)
        product = dot(
            feature_of(h),
            jnp.concatenate([kernels[slot][k] for k in range(bases)], axis=1),
            contract_rows,
        )
        message = product[:, :size] * radial_wide[0]
        for k in range(1, bases):
            message += product[:, k * size : (k + 1) * size] * radial_wide[k]
        total[g] += message

    pipelined(number, make, use)


def two_own_kernel(
    tiles, count, pack, own, radial_one, radial_two,
    total, wide_ext, radial_one_wide, radial_two_wide,
    kernel_a, kernel_b, order,
):
    extent, clusters = pack.shape[0], own.shape[0]
    margin = (extent - clusters) // 2
    for h in range(extent):
        wide_columns(pack[h], wide_ext, h)
    wide_radial(radial_one, radial_one_wide)
    wide_radial(radial_two, radial_two_wide)
    total[...] = jnp.zeros_like(total)
    number = select(
        tiles, count, order,
        lambda h: jnp.logical_and(h >= margin, h < margin + clusters),
    )
    layer_two_tiles(
        tiles, order, number, margin, wide_ext, pack,
        lambda h: own[jnp.clip(h - margin, 0, clusters - 1)],
        radial_two_wide, (kernel_a, kernel_b), None, total,
    )


def two_halo_kernel(
    tiles, count, pack, left, right, own, mix, readout, wide_ext, radial_wide, total_own,
    energy_out, adjoint_out, weighted, back_left, back_right,
    halo, kernel_a, kernel_b, kept, total, grad, order,
):
    clusters = own.shape[0]
    margin = left.shape[0]
    bases, channels, size = radial_wide.shape
    for s in range(margin):
        halo[s] = left[s]
        halo[margin + s] = right[s]
    total[...] = jnp.zeros_like(total)
    grad[...] = jnp.zeros_like(grad)
    number = select(
        tiles, count, order,
        lambda h: jnp.logical_or(h < margin, h >= margin + clusters),
    )
    layer_two_tiles(
        tiles, order, number, margin, wide_ext, pack,
        lambda h: halo[halo_slot(h, margin, clusters)],
        radial_wide, (kernel_a, kernel_b), kept, total,
    )
    readout_wide = readout[...].astype(f32)
    for g in range(clusters):
        parts = [own[g, m * size : (m + 1) * size, :].astype(f32) for m in range(4)]
        act = dot(jnp.transpose(total[g] + total_own[g]).astype(bf16), mix[...])
        act = act + parts[0] + (parts[1] * parts[1] + parts[2] * parts[2] + parts[3] * parts[3])
        sig = 1.0 / (1.0 + jnp.exp(-act))
        energy_out[g : g + 1, :] = jnp.sum(
            jnp.transpose(act * sig * readout_wide), axis=0, keepdims=True
        )
        adjoint = readout_wide * sig * (1.0 + act * (1.0 - sig))
        adjoint_out[g] = adjoint
        high, low = split(adjoint)
        second = dot(mix[...], high, contract_cols) + dot(mix[...], low, contract_cols)
        for k in range(bases):
            weighted[g, k] = (second * radial_wide[k]).astype(bf16)

    def backward(i, carry):
        g, h, _, _ = tile_of(tiles, order, number, i, margin)
        grad[halo_slot(h, margin, clusters)] += dot(
            jnp.concatenate([weighted[g, k] for k in range(bases)], axis=1),
            jnp.concatenate([kept[i, k] for k in range(bases)], axis=1),
            contract_cols,
        )
        return carry

    lax.fori_loop(0, number, backward, 0)
    for s in range(margin):
        back_left[s] = grad[s].astype(bf16)
        back_right[s] = grad[margin + s].astype(bf16)


def two_back_kernel(
    tiles, count, pack, left, right, own, mix, adjoint, weighted, wide_ext,
    first_out, feature_out,
    kernel_a, kernel_b, grad, direct, order,
):
    clusters = own.shape[0]
    margin = left.shape[0]
    bases, channels, size = weighted.shape[1:]
    grad[...] = jnp.zeros_like(grad)
    for s in range(margin):
        feature_out[s] = left[s]
        feature_out[margin + clusters + s] = right[s]
    for g in range(clusters):
        feature_out[margin + g] = own[g]
    number = select(
        tiles, count, order,
        lambda h: jnp.logical_and(h >= margin, h < margin + clusters),
    )
    kernels = (kernel_a, kernel_b)

    def make(i, slot):
        g, h, shift, key = tile_of(tiles, order, number, i, margin)
        write_kernel(
            [writer(kernels[slot])], reader(wide_ext, h), pack[g + margin], True, shift, key, bases
        )

    def use(i, slot):
        g, h, _, _ = tile_of(tiles, order, number, i, margin)
        grad[jnp.clip(h - margin, 0, clusters - 1)] += dot(
            jnp.concatenate([weighted[g, k] for k in range(bases)], axis=1),
            jnp.concatenate([kernels[slot][k] for k in range(bases)], axis=1),
            contract_cols,
        )

    pipelined(number, make, use)
    for g in range(clusters):
        direct[:size, :] = adjoint[g]
        for m in range(1, 4):
            direct[m * size : (m + 1) * size, :] = (
                2.0 * own[g, m * size : (m + 1) * size, :].astype(f32) * adjoint[g]
            )
        high, low = split(direct[...])
        first = dot(mix[...], high, contract_cols) + dot(mix[...], low, contract_cols)
        high, low = split(grad[g])
        first_out[g] = first + (dot(mix[...], high) + dot(mix[...], low))


def force_kernel(
    tiles, count, border, pack, embedded, feature, first_own, from_left, from_right,
    radial_wide, mix, weighted_two, wide_ext,
    force_out, back_left, back_right,
    first, weighted_one, product_a, product_b, center_sum, partner_sum, order,
):
    clusters = first_own.shape[0]
    margin = from_left.shape[0]
    bases, channels, size = radial_wide.shape
    extent = clusters + 2 * margin
    ratios = steps_of(bases)
    for g in range(clusters):
        first[g] = first_own[g]
    for ref, side in ((from_left, 0), (from_right, 1)):
        for s in range(margin):
            first[border[side, s]] += dot(mix[...], ref[s])
    for start in range(0, channels, FINE):
        span = slice(start, start + FINE)
        scales = [radial_wide[k, span, :] for k in range(bases)]
        for g in range(clusters):
            for m in range(4):
                part = first[g, span, m * size : (m + 1) * size]
                for k in range(bases):
                    weighted_one[g, m, k, span, :] = (part * scales[k]).astype(bf16)
    center_sum[...] = jnp.zeros_like(center_sum)
    partner_sum[...] = jnp.zeros_like(partner_sum)
    number = select(tiles, count, order, lambda h: h >= 0)
    products = (product_a, product_b)

    def multiply(i, slot):
        g, h, _, _ = tile_of(tiles, order, number, i, margin)
        base = embedded[h]
        for m in range(4):
            given = jnp.concatenate([base, feature[h, m * size : (m + 1) * size, :]], axis=1)
            for k in range(0, bases, 2):
                pair = dot(
                    given,
                    jnp.concatenate(
                        [
                            jnp.concatenate([weighted_one[g, m, k], weighted_one[g, m, k + 1]], axis=1),
                            jnp.concatenate([weighted_two[g, k], weighted_two[g, k + 1]], axis=1),
                        ],
                        axis=0,
                    ),
                )
                products[slot][m, k] = pair[:, :size]
                products[slot][m, k + 1] = pair[:, size:]

    def gather(i, slot):
        g, h, shift, key = tile_of(tiles, order, number, i, margin)
        product = products[slot]
        row = pack[g + margin]
        rows = [row[e : e + 1, :] for e in range(3)]
        sums = [None] * 3
        for start in range(0, size, FINE):
            cols = [wide_ext[h, e, start : start + FINE, :] for e in range(3)]
            offset, inverse, shifted, fall, fall_masked, gauss, ratio = pair_geometry(
                cols, rows, True, shift, key, start
            )
            unit = [part * inverse for part in offset]
            basis = [gauss * fall_masked]
            for k in range(1, bases):
                basis.append(basis[-1] * (ratio * ratios[k - 1]))
            plain, slope = [], []
            for m in range(4):
                tail = None
                weigh = None
                for k in range(bases - 1, -1, -1):
                    term = basis[k] * product[m, k, start : start + FINE, :]
                    tail = term if tail is None else tail + term
                    if k:
                        weigh = tail if weigh is None else weigh + tail
                plain.append(tail)
                slope.append(weigh)
            scale0 = shifted * fall * (-2.0 / (spread * spread)) - (shifted + first_center) * (
                4.0 / (cutoff * cutoff)
            )
            scale1 = fall * (2.0 * center_step / (spread * spread))
            bent = unit[0] * plain[1] + unit[1] * plain[2] + unit[2] * plain[3]
            slope_sum = slope[0] + unit[0] * slope[1] + unit[1] * slope[2] + unit[2] * slope[3]
            near = fall * inverse
            along = scale0 * (plain[0] + bent) + scale1 * slope_sum - near * bent
            for e in range(3):
                move = unit[e] * along + near * plain[e + 1]
                partner_sum[h, e, start : start + FINE, :] += jnp.sum(move, axis=1, keepdims=True)
                part = move[:8]
                for r in range(8, FINE, 8):
                    part = part + move[r : r + 8]
                sums[e] = part if sums[e] is None else sums[e] + part
        for e in range(3):
            center_sum[g, e] += sums[e]

    pipelined(number, multiply, gather)
    lanes = lax.broadcasted_iota(jnp.int32, (size, ROWS), 1)
    lines = []
    for h in range(extent):
        total = [partner_sum[h, e] for e in range(3)]
        wide = jnp.where(lanes == 0, total[0], jnp.where(lanes == 1, total[1], total[2]))
        lines.append(jnp.transpose(wide))
    for g in range(clusters):
        for e in range(3):
            force_out[e, g : g + 1, :] = (
                jnp.sum(center_sum[g, e], axis=0, keepdims=True) - lines[g + margin][e : e + 1]
            )
    for s in range(margin):
        back_left[s] = -lines[s]
        back_right[s] = -lines[margin + clusters + s]


def finish_kernel(border, own, from_left, from_right, out):
    out[...] = own[...]
    for ref, side in ((from_left, 0), (from_right, 1)):
        for s in range(ref.shape[0]):
            place = pl.ds(border[side, s], 1)
            for e in range(3):
                out[e, place, :] += ref[s, e : e + 1, :]


smem = pl.BlockSpec(memory_space=pltpu.SMEM)
vmem = pl.BlockSpec(memory_space=pltpu.VMEM)


def call(body, name, n_scalar, n_vector, outs, scratch, mib, cost_us=1):
    return pl.pallas_call(
        body,
        name=name,
        out_shape=outs,
        in_specs=[smem] * n_scalar + [vmem] * n_vector,
        out_specs=[vmem] * len(outs),
        scratch_shapes=scratch,
        cost_estimate=pl.CostEstimate(
            flops=int(cost_us * 900e6), bytes_accessed=1 << 16, transcendentals=0
        ),
        compiler_params=pltpu.CompilerParams(vmem_limit_bytes=mib * 1024 * 1024),
    )


def swap(to_left, to_right, axis):
    count = lax.axis_size(axis)
    from_left = lax.ppermute(to_right, axis, [(i, (i + 1) % count) for i in range(count)])
    from_right = lax.ppermute(to_left, axis, [((i + 1) % count, i) for i in range(count)])
    return from_left, from_right


def shards(
    positions, species, element_embed, radial_one, mix_one, radial_two, mix_two, readout,
    tile_list, tile_count, border,
):
    clusters, _, size = positions.shape
    channels = element_embed.shape[1]
    bases = radial_one.shape[0]
    margin = border.shape[1]
    extent = clusters + 2 * margin
    slots = tile_list.shape[0]
    sds = jax.ShapeDtypeStruct
    buffer = pltpu.VMEM
    order = pltpu.SMEM((slots + 1,), jnp.int32)
    pair = [buffer((bases, 4 * size, size), bf16)] * 2
    tiles = tile_list.T
    wide = -(-element_embed.shape[0] // 128) * 128
    embed = jnp.pad(element_embed, ((0, wide - element_embed.shape[0]), (0, 0)))

    own, to_left, to_right = call(
        pack_kernel, "pack", 1, 2,
        [
            sds((clusters, ROWS, size), f32),
            sds((margin, ROWS, size), f32),
            sds((margin, ROWS, size), f32),
        ],
        [], 4,
    )(border, positions.transpose(1, 0, 2), species)
    pack_left, pack_right = swap(to_left, to_right, "bx")
    weights = [buffer((clusters, bases * size, channels), bf16)] * 2
    embedded_own, wide_own, total_own = call(
        lambda *refs: one_own_kernel(*refs, margin=margin), "one_own", 2, 3,
        [
            sds((clusters, size, channels), bf16),
            sds((clusters, 3, size, size), f32),
            sds((clusters, 4 * size, channels), f32),
        ],
        weights + pair + [order], 12, 4,
    )(tiles, tile_count, own, embed, radial_one)
    feature, to_left, to_right, pack_ext, embedded = call(
        one_halo_kernel, "one_halo", 3, 9,
        [
            sds((clusters, 4 * size, channels), bf16),
            sds((margin, 4 * size, channels), bf16),
            sds((margin, 4 * size, channels), bf16),
            sds((extent, ROWS, size), f32),
            sds((extent, size, channels), bf16),
        ],
        [buffer((2 * margin, bases * size, channels), bf16)] * 2
        + [buffer((2 * margin, ROWS, size), f32)]
        + pair
        + [buffer((clusters, 4 * size, channels), f32), order], 14, 4,
    )(
        tiles, tile_count, border, pack_left, pack_right, own, embed, radial_one, mix_one,
        embedded_own, wide_own, total_own,
    )
    feature_left, feature_right = swap(to_left, to_right, "bx")
    total_two, wide_ext, radial_one_wide, radial_two_wide = call(
        two_own_kernel, "two_own", 2, 4,
        [
            sds((clusters, channels, size), f32),
            sds((extent, 3, size, size), f32),
            sds((bases, channels, size), f32),
            sds((bases, channels, size), f32),
        ],
        pair + [order], 10, 4,
    )(tiles, tile_count, pack_ext, feature, radial_one, radial_two)
    energy, adjoint, weighted_two, back_left, back_right = call(
        two_halo_kernel, "two_halo", 2, 9,
        [
            sds((clusters, size), f32),
            sds((clusters, size, channels), f32),
            sds((clusters, bases, channels, size), bf16),
            sds((margin, channels, 4 * size), bf16),
            sds((margin, channels, 4 * size), bf16),
        ],
        [buffer((2 * margin, 4 * size, channels), bf16)]
        + pair
        + [
            buffer((slots + 2, bases, 4 * size, size), bf16),
            buffer((clusters, channels, size), f32),
            buffer((2 * margin, channels, 4 * size), f32),
            order,
        ], 26, 4,
    )(
        tiles, tile_count, pack_ext, feature_left, feature_right, feature, mix_two,
        readout.reshape(1, channels), wide_ext, radial_two_wide, total_two,
    )
    grad_left, grad_right = swap(back_left, back_right, "bx")
    first, feature_ext = call(
        two_back_kernel, "two_back", 2, 8,
        [
            sds((clusters, channels, 4 * size), f32),
            sds((extent, 4 * size, channels), bf16),
        ],
        pair
        + [
            buffer((clusters, channels, 4 * size), f32),
            buffer((4 * size, channels), f32),
            order,
        ], 12, 4,
    )(
        tiles, tile_count, pack_ext, feature_left, feature_right, feature, mix_one, adjoint,
        weighted_two, wide_ext,
    )
    force, move_left, move_right = call(
        force_kernel, "forces", 3, 10,
        [
            sds((3, clusters, size), f32),
            sds((margin, ROWS, size), f32),
            sds((margin, ROWS, size), f32),
        ],
        [
            buffer((clusters, channels, 4 * size), f32),
            buffer((clusters, 4, bases, channels, size), bf16),
            buffer((4, bases, size, size), f32),
            buffer((4, bases, size, size), f32),
            buffer((clusters, 3, 8, size), f32),
            buffer((extent, 3, size, 1), f32),
            order,
        ], 20, 4,
    )(
        tiles, tile_count, border, pack_ext, embedded, feature_ext, first, grad_left, grad_right,
        radial_one_wide, mix_one, weighted_two, wide_ext,
    )
    moved_left, moved_right = swap(move_left, move_right, "bx")
    forces = call(finish_kernel, "finish", 1, 3, [sds((3, clusters, size), f32)], [], 4)(
        border, force, moved_left, moved_right
    )[0]
    return (
        energy,
        forces.transpose(1, 0, 2),
        feature.reshape(clusters, 4, size, channels),
    )


def solution(mesh):
    placed = (
        P(("rep", "bx"), None, None),
        P(("rep", "bx"), None),
        P(),
        P(),
        P(),
        P(),
        P(),
        P(),
        P(("rep", "bx"), None),
        P(("rep", "bx")),
        P(("rep", "bx"), None),
    )
    return jax.shard_map(
        shards,
        mesh=mesh,
        in_specs=placed,
        out_specs=(
            P(("rep", "bx"), None),
            P(("rep", "bx"), None, None),
            P(("rep", "bx"), None, None, None),
        ),
        check_vma=False,
    )
```

```python
import math

import jax
import jax.numpy as jnp
from jax import lax
from jax.experimental import pallas as pl
from jax.experimental.pallas import tpu as pltpu
from jax.sharding import PartitionSpec as P

soften = 0.25
cutoff = 3.6
spread = 0.9
first_center = 0.25
center_step = 0.45
message_scale = 0.125
dead_shift = 60.0
f32 = jnp.float32
bf16 = jnp.bfloat16
STEP = 32
FINE = 16
FORCE_UNROLL = 4
ROWS = 8

contract_cols = (((1,), (1,)), ((), ()))
contract_rows = (((0,), (0,)), ((), ()))


def dot(left, right, dims=(((1,), (0,)), ((), ()))):
    return lax.dot_general(left, right, dims, preferred_element_type=f32)


def split(value):
    high = value.astype(bf16)
    return high, (value - high.astype(f32)).astype(bf16)


def wide_columns(pack, out_ref, at):
    size = pack.shape[-1]
    for e in range(3):
        out_ref[at, e] = jnp.transpose(jnp.broadcast_to(pack[e : e + 1, :], (size, size)))


def wide_radial(radial, out_ref):
    bases, channels = radial.shape
    for k in range(bases):
        out_ref[k] = jnp.transpose(
            jnp.broadcast_to(radial[k : k + 1, :] * message_scale, (channels, channels))
        )


def pair_geometry(cols, rows, partner_rows, shift, key, start):
    if partner_rows:
        offset = [col - row for row, col in zip(rows, cols)]
    else:
        offset = [row - col for row, col in zip(rows, cols)]
    square = offset[0] * offset[0] + offset[1] * offset[1] + (offset[2] * offset[2] + shift)
    inverse = lax.rsqrt(square)
    shifted = square * inverse - first_center
    fall = jnp.maximum(1.0 - square * (1.0 / (cutoff * cutoff)), 0.0)
    shape = cols[0].shape
    apart = lax.broadcasted_iota(jnp.int32, shape, 1) - lax.broadcasted_iota(jnp.int32, shape, 0)
    fall_masked = jnp.where(apart == key + start, 0.0, fall)
    scale = math.log2(math.e) / (spread * spread)
    gauss = jnp.exp2(shifted * shifted * -scale)
    ratio = jnp.exp2(shifted * (2.0 * center_step * scale))
    return offset, inverse, shifted, fall, fall_masked, gauss, ratio


def steps_of(bases):
    base = (center_step / spread) ** 2
    return [math.exp(-base * (2 * k - 1)) for k in range(1, bases)]


def select(tiles, count, order, keep):
    number = jnp.int32(0)
    slots = tiles.shape[0] // 2
    for t in range(slots):
        order[number] = t
        wanted = jnp.logical_and(t < count[0, 0], keep(tiles[slots + t]))
        number = number + wanted.astype(jnp.int32)
    return number


def tile_of(tiles, order, number, i, margin):
    t = order[jnp.maximum(jnp.minimum(i, number - 1), 0)]
    g, h = tiles[t], tiles[tiles.shape[0] // 2 + t]
    key = jnp.where(h == g + margin, 0, 1 << 20).astype(jnp.int32)
    shift = jnp.where(i < number, soften, soften + dead_shift).astype(f32)
    return g, h, shift, key


def weave(*streams):
    pieces = []
    for place, (count, stream) in enumerate(streams):
        pieces += [((i + 0.5) / count, place, stream) for i in range(count)]
    for _, _, stream in sorted(pieces, key=lambda piece: piece[:2]):
        next(stream)
    for _, stream in streams:
        assert next(stream, None) is None


def pipelined(number, first, first_pieces, second, second_pieces, unroll=2):
    @pl.when(number > 0)
    def _():
        weave((first_pieces, first(0, 0)))

        def step(i, carry):
            for j in range(unroll):
                at = unroll * i + j
                weave(
                    (second_pieces, second(at, j % 2)),
                    (first_pieces, first(at + 1, (j + 1) % 2)),
                )
            return carry

        lax.fori_loop(0, (number + unroll - 1) // unroll, step, 0)


def write_kernel(writers, wide, row, partner_rows, shift, key, bases):
    size = row.shape[-1]
    ratios = steps_of(bases)
    rows = [row[e : e + 1, :] for e in range(3)]
    for start in range(0, size, STEP):
        cols = [wide(e, start, STEP) for e in range(3)]
        offset, inverse, _, fall, fall_masked, gauss, ratio = pair_geometry(
            cols, rows, partner_rows, shift, key, start
        )
        unit = [part * inverse for part in offset]
        basis = gauss * fall * fall_masked
        for k in range(bases):
            if k:
                basis = basis * (ratio * ratios[k - 1])
            for m in range(4):
                value = (basis if m == 0 else basis * unit[m - 1]).astype(bf16)
                for write in writers:
                    write(k, slice(m * size + start, m * size + start + STEP), value)
        yield True


def writer(ref, *lead):
    def write(k, rows, value):
        ref[(*lead, k, rows)] = value

    return write


def reader(ref, at):
    return lambda e, start, step: ref[at, e, start : start + step, :]


def fill_pack(out, at, positions, species, g):
    out[at] = jnp.zeros(out.shape[1:], f32)
    for e in range(3):
        out[at, e : e + 1, :] = positions[e, pl.ds(g, 1), :]
    out[at, 3:4, :] = species[pl.ds(g, 1), :].astype(f32)


def pack_kernel(border, positions, species, left_out, right_out):
    for s in range(border.shape[1]):
        fill_pack(left_out, s, positions, species, border[0, s])
        fill_pack(right_out, s, positions, species, border[1, s])


def embed_cluster(pack, embed, radial, embedded_out, weighted, rest, at, out_at):
    size = pack.shape[-1]
    col = jnp.transpose(pack)
    onehot = (
        lax.broadcasted_iota(jnp.int32, (size, embed.shape[0]), 1).astype(f32) == col[:, 3:4]
    ).astype(bf16)
    wide = dot(onehot, embed[...])
    embedded_out[out_at] = wide.astype(bf16)
    for k in range(radial.shape[0]):
        high, low = split(wide * (message_scale * radial[k : k + 1, :]))
        weighted[at, k * size : (k + 1) * size, :] = high
        rest[at, k * size : (k + 1) * size, :] = low


def layer_one_tiles(
    tiles, order, number, margin, wide_own, row_of, weights_of, kernels, total, bases
):
    def make(i, slot):
        g, h, shift, key = tile_of(tiles, order, number, i, margin)
        yield from write_kernel(
            [writer(kernels[slot])], reader(wide_own, g), row_of(h), False, shift, key, bases
        )

    def use(i, slot):
        g, h, _, _ = tile_of(tiles, order, number, i, margin)
        size = total.shape[1] // 4
        weights = jnp.concatenate(weights_of(h), axis=1)
        for m in range(4):
            rows = slice(m * size, (m + 1) * size)
            both = dot(
                jnp.concatenate([kernels[slot][k, rows] for k in range(bases)], axis=1), weights
            )
            half = both.shape[1] // 2
            total[g, rows] += both[:, :half] + both[:, half:]
            yield True

    pipelined(number, make, wide_own.shape[2] // STEP, use, 4)


def one_own_kernel(
    tiles, count, positions, species, embed, radial,
    own, embedded_out, wide_own, total,
    weighted, rest, kernel_a, kernel_b, order, *, margin,
):
    clusters = own.shape[0]
    bases = radial.shape[0]
    for g in range(clusters):
        fill_pack(own, g, positions, species, g)
        wide_columns(own[g], wide_own, g)
        embed_cluster(own[g], embed, radial, embedded_out, weighted, rest, g, g)
    total[...] = jnp.zeros_like(total)
    number = select(
        tiles, count, order,
        lambda h: jnp.logical_and(h >= margin, h < margin + clusters),
    )
    layer_one_tiles(
        tiles, order, number, margin, wide_own,
        lambda h: own[jnp.clip(h - margin, 0, clusters - 1)],
        lambda h: [ref[jnp.clip(h - margin, 0, clusters - 1)] for ref in (weighted, rest)],
        (kernel_a, kernel_b), total, bases,
    )


def halo_slot(h, margin, clusters):
    return jnp.where(h < margin, h, jnp.maximum(h - clusters, 0))


def one_halo_kernel(
    tiles, count, border, left, right, own, embed, radial, mix, embedded_own, wide_own, total_own,
    feature_out, send_left, send_right, pack_out, embedded_out,
    weighted, rest, halo, kernel_a, kernel_b, total, order,
):
    clusters, _, size = own.shape
    margin = left.shape[0]
    bases = radial.shape[0]
    for s in range(margin):
        for at, ref, out_at in ((s, left, s), (margin + s, right, margin + clusters + s)):
            pack = ref[s]
            halo[at] = pack
            pack_out[out_at] = pack
            embed_cluster(pack, embed, radial, embedded_out, weighted, rest, at, out_at)
    for g in range(clusters):
        pack_out[margin + g] = own[g]
        embedded_out[margin + g] = embedded_own[g]
    total[...] = jnp.zeros_like(total)
    number = select(
        tiles, count, order,
        lambda h: jnp.logical_or(h < margin, h >= margin + clusters),
    )
    layer_one_tiles(
        tiles, order, number, margin, wide_own,
        lambda h: halo[halo_slot(h, margin, clusters)],
        lambda h: [ref[halo_slot(h, margin, clusters)] for ref in (weighted, rest)],
        (kernel_a, kernel_b), total, bases,
    )
    for g in range(clusters):
        mixed = dot((total[g] + total_own[g]).astype(bf16), mix[...])
        for m in range(4):
            part = mixed[m * size : (m + 1) * size]
            if m == 0:
                part = part + embedded_own[g].astype(f32)
            feature_out[g, m * size : (m + 1) * size, :] = part.astype(bf16)
    for s in range(margin):
        send_left[s] = feature_out[border[s]]
        send_right[s] = feature_out[border[margin + s]]


def layer_two_tiles(
    tiles, order, number, margin, wide_ext, pack, feature_of, radial_wide, kernels, kept, total
):
    bases = radial_wide.shape[0]
    size = pack.shape[-1]

    def make(i, slot):
        g, h, shift, key = tile_of(tiles, order, number, i, margin)
        writers = [writer(kernels[slot])]
        if kept is not None:
            writers.append(writer(kept, i))
        yield from write_kernel(writers, reader(wide_ext, h), pack[g + margin], True, shift, key, bases)

    def use(i, slot):
        g, h, _, _ = tile_of(tiles, order, number, i, margin)
        channel_rows = jnp.transpose(feature_of(h))
        message = None
        for k in range(0, bases, 2):
            product = dot(
                channel_rows, jnp.concatenate([kernels[slot][k], kernels[slot][k + 1]], axis=1)
            )
            for j in range(2):
                term = product[:, j * size : (j + 1) * size] * radial_wide[k + j]
                message = term if message is None else message + term
            if k == bases - 2:
                total[g] += message
            yield True

    pipelined(number, make, size // STEP, use, bases // 2)


def two_own_kernel(
    tiles, count, pack, own, radial_one, radial_two,
    total, wide_ext, radial_one_wide, radial_two_wide, descriptors,
    kernel_a, kernel_b, order, sem,
):
    copy = pltpu.make_async_copy(own, descriptors, sem)
    copy.start()
    extent, clusters = pack.shape[0], own.shape[0]
    margin = (extent - clusters) // 2
    for h in range(extent):
        wide_columns(pack[h], wide_ext, h)
    wide_radial(radial_one, radial_one_wide)
    wide_radial(radial_two, radial_two_wide)
    total[...] = jnp.zeros_like(total)
    number = select(
        tiles, count, order,
        lambda h: jnp.logical_and(h >= margin, h < margin + clusters),
    )
    layer_two_tiles(
        tiles, order, number, margin, wide_ext, pack,
        lambda h: own[jnp.clip(h - margin, 0, clusters - 1)],
        radial_two_wide, (kernel_a, kernel_b), None, total,
    )
    copy.wait()


def two_halo_kernel(
    tiles, count, pack, left, right, own, mix, readout, wide_ext, radial_wide, total_own,
    energy_out, adjoint_out, weighted, back_left, back_right,
    halo, kernel_a, kernel_b, kept, total, grad, order,
):
    clusters = own.shape[0]
    margin = left.shape[0]
    bases, channels, size = radial_wide.shape
    for s in range(margin):
        halo[s] = left[s]
        halo[margin + s] = right[s]
    total[...] = jnp.zeros_like(total)
    grad[...] = jnp.zeros_like(grad)
    number = select(
        tiles, count, order,
        lambda h: jnp.logical_or(h < margin, h >= margin + clusters),
    )
    layer_two_tiles(
        tiles, order, number, margin, wide_ext, pack,
        lambda h: halo[halo_slot(h, margin, clusters)],
        radial_wide, (kernel_a, kernel_b), kept, total,
    )
    readout_wide = readout[...].astype(f32)
    for g in range(clusters):
        parts = [own[g, m * size : (m + 1) * size, :].astype(f32) for m in range(4)]
        act = dot(jnp.transpose(total[g] + total_own[g]).astype(bf16), mix[...])
        act = act + parts[0] + (parts[1] * parts[1] + parts[2] * parts[2] + parts[3] * parts[3])
        sig = 1.0 / (1.0 + jnp.exp(-act))
        energy_out[g : g + 1, :] = jnp.sum(
            jnp.transpose(act * sig * readout_wide), axis=0, keepdims=True
        )
        adjoint = readout_wide * sig * (1.0 + act * (1.0 - sig))
        adjoint_out[g] = adjoint
        high, low = split(adjoint)
        second = dot(mix[...], high, contract_cols) + dot(mix[...], low, contract_cols)
        for k in range(bases):
            weighted[g, k] = (second * radial_wide[k]).astype(bf16)

    def backward(i, carry):
        g, h, _, _ = tile_of(tiles, order, number, i, margin)
        grad[halo_slot(h, margin, clusters)] += dot(
            jnp.concatenate([weighted[g, k] for k in range(bases)], axis=1),
            jnp.concatenate([kept[i, k] for k in range(bases)], axis=1),
            contract_cols,
        )
        return carry

    lax.fori_loop(0, number, backward, 0)
    for s in range(margin):
        back_left[s] = grad[s].astype(bf16)
        back_right[s] = grad[margin + s].astype(bf16)


def two_back_kernel(
    tiles, count, pack, left, right, own, mix, adjoint, weighted, wide_ext, energy,
    first_out, feature_out, energy_out,
    kernel_a, kernel_b, grad, direct, order, sem,
):
    copy = pltpu.make_async_copy(energy, energy_out, sem)
    copy.start()
    clusters = own.shape[0]
    margin = left.shape[0]
    bases, channels, size = weighted.shape[1:]
    grad[...] = jnp.zeros_like(grad)
    for s in range(margin):
        feature_out[s] = left[s]
        feature_out[margin + clusters + s] = right[s]
    for g in range(clusters):
        feature_out[margin + g] = own[g]
    number = select(
        tiles, count, order,
        lambda h: jnp.logical_and(h >= margin, h < margin + clusters),
    )
    kernels = (kernel_a, kernel_b)

    def make(i, slot):
        g, h, shift, key = tile_of(tiles, order, number, i, margin)
        yield from write_kernel(
            [writer(kernels[slot])], reader(wide_ext, h), pack[g + margin], True, shift, key, bases
        )

    def use(i, slot):
        g, h, _, _ = tile_of(tiles, order, number, i, margin)
        given = jnp.concatenate([weighted[g, k] for k in range(bases)], axis=1)
        for half in range(2):
            span = slice(half * 2 * size, (half + 1) * 2 * size)
            grad[jnp.clip(h - margin, 0, clusters - 1), :, span] += dot(
                given,
                jnp.concatenate([kernels[slot][k, span] for k in range(bases)], axis=1),
                contract_cols,
            )
            yield True

    pipelined(number, make, size // STEP, use, 2)
    for g in range(clusters):
        direct[:size, :] = adjoint[g]
        for m in range(1, 4):
            direct[m * size : (m + 1) * size, :] = (
                2.0 * own[g, m * size : (m + 1) * size, :].astype(f32) * adjoint[g]
            )
        high, low = split(direct[...])
        first = dot(mix[...], high, contract_cols) + dot(mix[...], low, contract_cols)
        high, low = split(grad[g])
        first_out[g] = first + (dot(mix[...], high) + dot(mix[...], low))
    copy.wait()


def force_kernel(
    tiles, count, border, pack, embedded, feature, first_own, from_left, from_right,
    radial_wide, mix, weighted_two, wide_ext,
    force_out, back_left, back_right,
    first, weighted_one, product_a, product_b, center_sum, partner_sum, returned, order,
):
    clusters = first_own.shape[0]
    margin = from_left.shape[0]
    bases, channels, size = radial_wide.shape
    extent = clusters + 2 * margin
    ratios = steps_of(bases)
    for s in range(margin):
        returned[s] = dot(mix[...], from_left[s])
        returned[margin + s] = dot(mix[...], from_right[s])
    for g in range(clusters):
        first[g] = first_own[g]
    for s in range(2 * margin):
        first[border[s]] += returned[s]
    for start in range(0, channels, FINE):
        span = slice(start, start + FINE)
        scales = [radial_wide[k, span, :] for k in range(bases)]
        for g in range(clusters):
            for m in range(4):
                part = first[g, span, m * size : (m + 1) * size]
                for k in range(bases):
                    weighted_one[g, m, k, span, :] = (part * scales[k]).astype(bf16)
    center_sum[...] = jnp.zeros_like(center_sum)
    partner_sum[...] = jnp.zeros_like(partner_sum)
    number = select(tiles, count, order, lambda h: h >= 0)
    products = (product_a, product_b)

    def multiply(i, slot):
        g, h, _, _ = tile_of(tiles, order, number, i, margin)
        base = embedded[h]
        for m in range(4):
            given = jnp.concatenate([base, feature[h, m * size : (m + 1) * size, :]], axis=1)
            for k in range(0, bases, 2):
                pair = dot(
                    given,
                    jnp.concatenate(
                        [
                            jnp.concatenate([weighted_one[g, m, k], weighted_one[g, m, k + 1]], axis=1),
                            jnp.concatenate([weighted_two[g, k], weighted_two[g, k + 1]], axis=1),
                        ],
                        axis=0,
                    ),
                )
                products[slot][m, k] = pair[:, :size]
                products[slot][m, k + 1] = pair[:, size:]
                yield True

    def gather(i, slot):
        g, h, shift, key = tile_of(tiles, order, number, i, margin)
        product = products[slot]
        row = pack[g + margin]
        rows = [row[e : e + 1, :] for e in range(3)]
        sums = [None] * 3
        for start in range(0, size, FINE):
            cols = [wide_ext[h, e, start : start + FINE, :] for e in range(3)]
            offset, inverse, shifted, fall, fall_masked, gauss, ratio = pair_geometry(
                cols, rows, True, shift, key, start
            )
            unit = [part * inverse for part in offset]
            basis = [gauss * fall_masked]
            for k in range(1, bases):
                basis.append(basis[-1] * (ratio * ratios[k - 1]))
            plain, slope = [], []
            for m in range(4):
                tail = None
                weigh = None
                for k in range(bases - 1, -1, -1):
                    term = basis[k] * product[m, k, start : start + FINE, :]
                    tail = term if tail is None else tail + term
                    if k:
                        weigh = tail if weigh is None else weigh + tail
                plain.append(tail)
                slope.append(weigh)
            scale0 = shifted * fall * (-2.0 / (spread * spread)) - (shifted + first_center) * (
                4.0 / (cutoff * cutoff)
            )
            scale1 = fall * (2.0 * center_step / (spread * spread))
            bent = unit[0] * plain[1] + unit[1] * plain[2] + unit[2] * plain[3]
            slope_sum = slope[0] + unit[0] * slope[1] + unit[1] * slope[2] + unit[2] * slope[3]
            near = fall * inverse
            along = scale0 * (plain[0] + bent) + scale1 * slope_sum - near * bent
            lanes = lax.broadcasted_iota(jnp.int32, (FINE, size), 1)
            column = None
            for e in range(3):
                move = unit[e] * along + near * plain[e + 1]
                line = jnp.sum(move, axis=1, keepdims=True)
                column = line if column is None else jnp.where(lanes == e, line, column)
                part = move[:8]
                for r in range(8, FINE, 8):
                    part = part + move[r : r + 8]
                sums[e] = part if sums[e] is None else sums[e] + part
            partner_sum[h, start : start + FINE, :] += column
            if start + FINE == size:
                for e in range(3):
                    center_sum[g, e] += sums[e]
            yield True

    pipelined(number, multiply, 2 * bases, gather, size // FINE, unroll=FORCE_UNROLL)
    lines = [jnp.transpose(partner_sum[h]) for h in range(extent)]
    for g in range(clusters):
        for e in range(3):
            force_out[e, g : g + 1, :] = (
                jnp.sum(center_sum[g, e], axis=0, keepdims=True) - lines[g + margin][e : e + 1]
            )
    for s in range(margin):
        back_left[s] = -lines[s][:ROWS]
        back_right[s] = -lines[margin + clusters + s][:ROWS]


def finish_kernel(border, own, from_left, from_right, out):
    out[...] = own[...]
    for ref, side in ((from_left, 0), (from_right, 1)):
        for s in range(ref.shape[0]):
            place = pl.ds(border[side * ref.shape[0] + s], 1)
            for e in range(3):
                out[e, place, :] += ref[s, e : e + 1, :]


smem = pl.BlockSpec(memory_space=pltpu.SMEM)
vmem = pl.BlockSpec(memory_space=pltpu.VMEM)


hbm = pl.BlockSpec(memory_space=pltpu.HBM)


def call(body, name, ins, outs, scratch, mib, cost_us=1, last_out=0, flags=None):
    return pl.pallas_call(
        body,
        name=name,
        out_shape=outs,
        in_specs=ins,
        out_specs=[vmem] * (len(outs) - last_out) + [hbm] * last_out,
        scratch_shapes=scratch,
        cost_estimate=pl.CostEstimate(
            flops=int(cost_us * 900e6), bytes_accessed=1 << 16, transcendentals=0
        ),
        compiler_params=pltpu.CompilerParams(vmem_limit_bytes=mib * 1024 * 1024, flags=flags),
    )


def swap(to_left, to_right, axis):
    count = lax.axis_size(axis)
    from_left = lax.ppermute(to_right, axis, [(i, (i + 1) % count) for i in range(count)])
    from_right = lax.ppermute(to_left, axis, [((i + 1) % count, i) for i in range(count)])
    return from_left, from_right


def shards(
    positions, species, element_embed, radial_one, mix_one, radial_two, mix_two, readout,
    tile_list, tile_count, border,
):
    clusters, _, size = positions.shape
    channels = element_embed.shape[1]
    bases = radial_one.shape[0]
    margin = border.shape[1]
    extent = clusters + 2 * margin
    slots = tile_list.shape[0]
    sds = jax.ShapeDtypeStruct
    buffer = pltpu.VMEM
    order = pltpu.SMEM((slots + 1,), jnp.int32)
    pair = [buffer((bases, 4 * size, size), bf16)] * 2
    tiles = tile_list.T.reshape(-1)
    border_flat = border.reshape(-1)
    tile_count = tile_count.reshape(1, 1)
    wide = -(-element_embed.shape[0] // 128) * 128
    embed = jnp.pad(element_embed, ((0, wide - element_embed.shape[0]), (0, 0)))

    positions = positions.transpose(1, 0, 2)
    to_left, to_right = call(
        pack_kernel, "pack", [smem, vmem, vmem], [sds((margin, ROWS, size), f32)] * 2, [], 62
    )(border, positions, species)
    pack_left, pack_right = swap(to_left, to_right, "bx")
    weights = [buffer((clusters, bases * size, channels), bf16)] * 2
    own, embedded_own, wide_own, total_own = call(
        lambda *refs: one_own_kernel(*refs, margin=margin), "one_own", [smem] * 2 + [vmem] * 4,
        [
            sds((clusters, ROWS, size), f32),
            sds((clusters, size, channels), bf16),
            sds((clusters, 3, size, size), f32),
            sds((clusters, 4 * size, channels), f32),
        ],
        weights + pair + [order], 12, 4,
    )(tiles, tile_count, positions, species, embed, radial_one)
    feature, to_left, to_right, pack_ext, embedded = call(
        one_halo_kernel, "one_halo", [smem] * 3 + [vmem] * 9,
        [
            sds((clusters, 4 * size, channels), bf16),
            sds((margin, 4 * size, channels), bf16),
            sds((margin, 4 * size, channels), bf16),
            sds((extent, ROWS, size), f32),
            sds((extent, size, channels), bf16),
        ],
        [buffer((2 * margin, bases * size, channels), bf16)] * 2
        + [buffer((2 * margin, ROWS, size), f32)]
        + pair
        + [buffer((clusters, 4 * size, channels), f32), order], 14, 4,
    )(
        tiles, tile_count, border_flat, pack_left, pack_right, own, embed, radial_one, mix_one,
        embedded_own, wide_own, total_own,
    )
    feature_left, feature_right = swap(to_left, to_right, "bx")
    total_two, wide_ext, radial_one_wide, radial_two_wide, descriptors = call(
        two_own_kernel, "two_own", [smem] * 2 + [vmem] * 4,
        [
            sds((clusters, channels, size), f32),
            sds((extent, 3, size, size), f32),
            sds((bases, channels, size), f32),
            sds((bases, channels, size), f32),
            sds((clusters, 4 * size, channels), bf16),
        ],
        pair + [order, pltpu.SemaphoreType.DMA], 10, 4, 1,
    )(tiles, tile_count, pack_ext, feature, radial_one, radial_two)
    energy, adjoint, weighted_two, back_left, back_right = call(
        two_halo_kernel, "two_halo", [smem] * 2 + [vmem] * 9,
        [
            sds((clusters, size), f32),
            sds((clusters, size, channels), f32),
            sds((clusters, bases, channels, size), bf16),
            sds((margin, channels, 4 * size), bf16),
            sds((margin, channels, 4 * size), bf16),
        ],
        [buffer((2 * margin, 4 * size, channels), bf16)]
        + pair
        + [
            buffer((slots + 2, bases, 4 * size, size), bf16),
            buffer((clusters, channels, size), f32),
            buffer((2 * margin, channels, 4 * size), f32),
            order,
        ], 26, 4,
    )(
        tiles, tile_count, pack_ext, feature_left, feature_right, feature, mix_two,
        readout.reshape(1, channels), wide_ext, radial_two_wide, total_two,
    )
    grad_left, grad_right = swap(back_left, back_right, "bx")
    first, feature_ext, atom_energy = call(
        two_back_kernel, "two_back", [smem] * 2 + [vmem] * 9,
        [
            sds((clusters, channels, 4 * size), f32),
            sds((extent, 4 * size, channels), bf16),
            sds((clusters, size), f32),
        ],
        pair
        + [
            buffer((clusters, channels, 4 * size), f32),
            buffer((4 * size, channels), f32),
            order,
            pltpu.SemaphoreType.DMA,
        ], 12, 4, 1,
    )(
        tiles, tile_count, pack_ext, feature_left, feature_right, feature, mix_one, adjoint,
        weighted_two, wide_ext, energy,
    )
    force, move_left, move_right = call(
        force_kernel, "forces", [smem] * 3 + [vmem] * 10,
        [
            sds((3, clusters, size), f32),
            sds((margin, ROWS, size), f32),
            sds((margin, ROWS, size), f32),
        ],
        [
            buffer((clusters, channels, 4 * size), f32),
            buffer((clusters, 4, bases, channels, size), bf16),
            buffer((4, bases, size, size), f32),
            buffer((4, bases, size, size), f32),
            buffer((clusters, 3, 8, size), f32),
            buffer((extent, size, size), f32),
            buffer((2 * margin, channels, 4 * size), f32),
            order,
        ], 20, 4,
    )(
        tiles, tile_count, border_flat, pack_ext, embedded, feature_ext, first, grad_left, grad_right,
        radial_one_wide, mix_one, weighted_two, wide_ext,
    )
    moved_left, moved_right = swap(move_left, move_right, "bx")
    forces = call(finish_kernel, "finish", [smem] * 1 + [vmem] * 3, [sds((3, clusters, size), f32)], [], 4)(
        border_flat, force, moved_left, moved_right
    )[0]
    return (
        atom_energy,
        forces.transpose(1, 0, 2),
        descriptors.reshape(clusters, 4, size, channels),
    )


def solution(mesh):
    placed = (
        P(("rep", "bx"), None, None),
        P(("rep", "bx"), None),
        P(),
        P(),
        P(),
        P(),
        P(),
        P(),
        P(("rep", "bx"), None),
        P(("rep", "bx")),
        P(("rep", "bx"), None),
    )
    return jax.shard_map(
        shards,
        mesh=mesh,
        in_specs=placed,
        out_specs=(
            P(("rep", "bx"), None),
            P(("rep", "bx"), None, None),
            P(("rep", "bx"), None, None, None),
        ),
        check_vma=False,
    )
```

```python
import math

import jax
import jax.numpy as jnp
from jax import lax
from jax.experimental import pallas as pl
from jax.experimental.pallas import tpu as pltpu
from jax.sharding import PartitionSpec as P

soften = 0.25
cutoff = 3.6
spread = 0.9
first_center = 0.25
center_step = 0.45
message_scale = 0.125
dead_shift = 60.0
f32 = jnp.float32
bf16 = jnp.bfloat16
STEP = 32
FINE = 16
FORCE_UNROLL = 4
ROWS = 8

contract_cols = (((1,), (1,)), ((), ()))
contract_rows = (((0,), (0,)), ((), ()))


def dot(left, right, dims=(((1,), (0,)), ((), ()))):
    return lax.dot_general(left, right, dims, preferred_element_type=f32)


def split(value):
    high = value.astype(bf16)
    return high, (value - high.astype(f32)).astype(bf16)


def wide_columns(pack, out_ref, at):
    size = pack.shape[-1]
    for e in range(3):
        out_ref[at, e] = jnp.transpose(jnp.broadcast_to(pack[e : e + 1, :], (size, size)))


def wide_radial(radial, out_ref):
    bases, channels = radial.shape
    for k in range(bases):
        out_ref[k] = jnp.transpose(
            jnp.broadcast_to(radial[k : k + 1, :] * message_scale, (channels, channels))
        )


def pair_geometry(cols, rows, partner_rows, shift, key, start):
    if partner_rows:
        offset = [col - row for row, col in zip(rows, cols)]
    else:
        offset = [row - col for row, col in zip(rows, cols)]
    square = offset[0] * offset[0] + offset[1] * offset[1] + (offset[2] * offset[2] + shift)
    inverse = lax.rsqrt(square)
    shifted = square * inverse - first_center
    fall = jnp.maximum(1.0 - square * (1.0 / (cutoff * cutoff)), 0.0)
    shape = cols[0].shape
    apart = lax.broadcasted_iota(jnp.int32, shape, 1) - lax.broadcasted_iota(jnp.int32, shape, 0)
    fall_masked = jnp.where(apart == key + start, 0.0, fall)
    scale = math.log2(math.e) / (spread * spread)
    gauss = jnp.exp2(shifted * shifted * -scale)
    ratio = jnp.exp2(shifted * (2.0 * center_step * scale))
    return offset, inverse, shifted, fall, fall_masked, gauss, ratio


def steps_of(bases):
    base = (center_step / spread) ** 2
    return [math.exp(-base * (2 * k - 1)) for k in range(1, bases)]


class View:
    def __init__(self, ref, start, length):
        self.ref, self.start, self.shape = ref, start, (length,)

    def __getitem__(self, at):
        return self.ref[self.start + at]


def select(tiles, count, order, keep):
    number = jnp.int32(0)
    slots = tiles.shape[0] // 2
    for t in range(slots):
        order[number] = t
        wanted = jnp.logical_and(t < count[0], keep(tiles[slots + t]))
        number = number + wanted.astype(jnp.int32)
    return number


def tile_of(tiles, order, number, i, margin):
    t = order[jnp.maximum(jnp.minimum(i, number - 1), 0)]
    g, h = tiles[t], tiles[tiles.shape[0] // 2 + t]
    key = jnp.where(h == g + margin, 0, 1 << 20).astype(jnp.int32)
    shift = jnp.where(i < number, soften, soften + dead_shift).astype(f32)
    return g, h, shift, key


def weave(*streams):
    pieces = []
    for place, (count, stream) in enumerate(streams):
        pieces += [((i + 0.5) / count, place, stream) for i in range(count)]
    for _, _, stream in sorted(pieces, key=lambda piece: piece[:2]):
        next(stream)
    for _, stream in streams:
        assert next(stream, None) is None


def pipelined(number, first, first_pieces, second, second_pieces, unroll=2, tail=True):
    def step(i, carry):
        for j in range(unroll):
            at = unroll * i + j
            weave(
                (second_pieces, second(at, j % 2)),
                (first_pieces, first(at + 1, (j + 1) % 2)),
            )
        return carry

    @pl.when(number > 0)
    def _():
        weave((first_pieces, first(0, 0)))
        if not tail:
            lax.fori_loop(0, (number + unroll - 1) // unroll, step, 0)
            return
        assert unroll == 2
        lax.fori_loop(0, number // 2, step, 0)

        @pl.when(number % 2 == 1)
        def _():
            weave((second_pieces, second(number - 1, 0)))


def write_kernel(out, wide, row, partner_rows, shift, key, bases):
    size = row.shape[-1]
    ratios = steps_of(bases)
    rows = [row[e : e + 1, :] for e in range(3)]
    for start in range(0, size, STEP):
        cols = [wide(e, start, STEP) for e in range(3)]
        offset, inverse, _, fall, fall_masked, gauss, ratio = pair_geometry(
            cols, rows, partner_rows, shift, key, start
        )
        unit = [part * inverse for part in offset]
        basis = gauss * fall * fall_masked
        for k in range(bases):
            if k:
                basis = basis * (ratio * ratios[k - 1])
            for m in range(4):
                value = (basis if m == 0 else basis * unit[m - 1]).astype(bf16)
                out[k, m * size + start : m * size + start + STEP, :] = value
        yield True


def reader(ref, at):
    return lambda e, start, step: ref[at, e, start : start + step, :]


def fill_pack(out, at, positions, species, g):
    out[at] = jnp.zeros(out.shape[1:], f32)
    for e in range(3):
        out[at, e : e + 1, :] = positions[e, pl.ds(g, 1), :]
    out[at, 3:4, :] = species[pl.ds(g, 1), :].astype(f32)


def pack_kernel(border, positions, species, left_out, right_out):
    for s in range(border.shape[1]):
        fill_pack(left_out, s, positions, species, border[0, s])
        fill_pack(right_out, s, positions, species, border[1, s])


def embed_cluster(pack, embed, radial, embedded_out, weighted, rest, at, out_at):
    size = pack.shape[-1]
    col = jnp.transpose(pack)
    onehot = (
        lax.broadcasted_iota(jnp.int32, (size, embed.shape[0]), 1).astype(f32) == col[:, 3:4]
    ).astype(bf16)
    wide = dot(onehot, embed[...])
    embedded_out[out_at] = wide.astype(bf16)
    for k in range(radial.shape[0]):
        high, low = split(wide * (message_scale * radial[k : k + 1, :]))
        weighted[at, k * size : (k + 1) * size, :] = high
        rest[at, k * size : (k + 1) * size, :] = low


def layer_one_tiles(
    tiles, order, number, margin, wide_own, row_of, weights_of, kernels, total, bases
):
    def make(i, slot):
        g, h, shift, key = tile_of(tiles, order, number, i, margin)
        yield from write_kernel(
            kernels[slot], reader(wide_own, g), row_of(h), False, shift, key, bases
        )

    def use(i, slot):
        g, h, _, _ = tile_of(tiles, order, number, i, margin)
        size = total.shape[1] // 4
        weights = jnp.concatenate(weights_of(h), axis=1)
        for m in range(4):
            rows = slice(m * size, (m + 1) * size)
            both = dot(
                jnp.concatenate([kernels[slot][k, rows] for k in range(bases)], axis=1), weights
            )
            half = both.shape[1] // 2
            total[g, rows] += both[:, :half] + both[:, half:]
            yield True

    pipelined(number, make, wide_own.shape[2] // STEP, use, 4)


def one_own_kernel(
    tiles, count, positions, species, embed, radial,
    own, embedded_out, wide_own, total,
    weighted, rest, kernel_a, kernel_b, order, *, margin,
):
    clusters = own.shape[0]
    bases = radial.shape[0]
    for g in range(clusters):
        fill_pack(own, g, positions, species, g)
        wide_columns(own[g], wide_own, g)
        embed_cluster(own[g], embed, radial, embedded_out, weighted, rest, g, g)
    total[...] = jnp.zeros_like(total)
    number = select(
        tiles, count, order,
        lambda h: jnp.logical_and(h >= margin, h < margin + clusters),
    )
    layer_one_tiles(
        tiles, order, number, margin, wide_own,
        lambda h: own[jnp.clip(h - margin, 0, clusters - 1)],
        lambda h: [ref[jnp.clip(h - margin, 0, clusters - 1)] for ref in (weighted, rest)],
        (kernel_a, kernel_b), total, bases,
    )


def halo_slot(h, margin, clusters):
    return jnp.where(h < margin, h, jnp.maximum(h - clusters, 0))


def one_halo_kernel(
    tiles, count, border, left, right, own, embed, radial, mix, embedded_own, wide_own, total_own,
    feature_out, send_left, send_right, pack_out, embedded_out,
    weighted, rest, halo, kernel_a, kernel_b, total, order,
):
    clusters, _, size = own.shape
    margin = left.shape[0]
    bases = radial.shape[0]
    for s in range(margin):
        for at, ref, out_at in ((s, left, s), (margin + s, right, margin + clusters + s)):
            pack = ref[s]
            halo[at] = pack
            pack_out[out_at] = pack
            embed_cluster(pack, embed, radial, embedded_out, weighted, rest, at, out_at)
    for g in range(clusters):
        pack_out[margin + g] = own[g]
        embedded_out[margin + g] = embedded_own[g]
    total[...] = jnp.zeros_like(total)
    number = select(
        tiles, count, order,
        lambda h: jnp.logical_or(h < margin, h >= margin + clusters),
    )
    layer_one_tiles(
        tiles, order, number, margin, wide_own,
        lambda h: halo[halo_slot(h, margin, clusters)],
        lambda h: [ref[halo_slot(h, margin, clusters)] for ref in (weighted, rest)],
        (kernel_a, kernel_b), total, bases,
    )
    for g in range(clusters):
        mixed = dot((total[g] + total_own[g]).astype(bf16), mix[...])
        for m in range(4):
            part = mixed[m * size : (m + 1) * size]
            if m == 0:
                part = part + embedded_own[g].astype(f32)
            feature_out[g, m * size : (m + 1) * size, :] = part.astype(bf16)
    for s in range(margin):
        send_left[s] = feature_out[border[s]]
        send_right[s] = feature_out[border[margin + s]]


def layer_two_tiles(
    tiles, order, number, margin, wide_ext, pack, feature_of, radial_wide, kernels, total
):
    bases = radial_wide.shape[0]
    size = pack.shape[-1]

    def make(i, slot):
        g, h, shift, key = tile_of(tiles, order, number, i, margin)
        yield from write_kernel(
            kernels[slot], reader(wide_ext, h), pack[g + margin], True, shift, key, bases
        )

    def use(i, slot):
        g, h, _, _ = tile_of(tiles, order, number, i, margin)
        channel_rows = jnp.transpose(feature_of(h))
        message = None
        for k in range(0, bases, 2):
            product = dot(
                channel_rows, jnp.concatenate([kernels[slot][k], kernels[slot][k + 1]], axis=1)
            )
            for j in range(2):
                term = product[:, j * size : (j + 1) * size] * radial_wide[k + j]
                message = term if message is None else message + term
            if k == bases - 2:
                total[g] += message
            yield True

    pipelined(number, make, size // STEP, use, bases // 2)


def two_own_kernel(
    tiles, count, pack, own, radial_one, radial_two,
    total, wide_ext, radial_one_wide, radial_two_wide, descriptors,
    kernel_a, kernel_b, order, sem,
):
    copy = pltpu.make_async_copy(own, descriptors, sem)
    copy.start()
    extent, clusters = pack.shape[0], own.shape[0]
    margin = (extent - clusters) // 2
    for h in range(extent):
        wide_columns(pack[h], wide_ext, h)
    wide_radial(radial_one, radial_one_wide)
    wide_radial(radial_two, radial_two_wide)
    total[...] = jnp.zeros_like(total)
    number = select(
        tiles, count, order,
        lambda h: jnp.logical_and(h >= margin, h < margin + clusters),
    )
    layer_two_tiles(
        tiles, order, number, margin, wide_ext, pack,
        lambda h: own[jnp.clip(h - margin, 0, clusters - 1)],
        radial_two_wide, (kernel_a, kernel_b), total,
    )
    copy.wait()


def back_tiles(
    tiles, order, number, margin, wide_ext, pack, weighted, kernels, grad, place_of
):
    bases, _, size = weighted.shape[1:]

    def make(i, slot):
        g, h, shift, key = tile_of(tiles, order, number, i, margin)
        yield from write_kernel(
            kernels[slot], reader(wide_ext, g + margin), pack[h], False, shift, key, bases
        )

    def use(i, slot):
        g, h, _, _ = tile_of(tiles, order, number, i, margin)
        given = jnp.concatenate([weighted[g, k] for k in range(bases)], axis=1)
        for m in range(0, 4, 2):
            one, two = (slice((m + j) * size, (m + j + 1) * size) for j in range(2))
            grad[place_of(h), :, m * size : (m + 2) * size] += dot(
                given,
                jnp.concatenate(
                    [
                        jnp.concatenate([kernels[slot][k, one], kernels[slot][k, two]], axis=1)
                        for k in range(bases)
                    ],
                    axis=0,
                ),
            )
            yield True

    pipelined(number, make, size // STEP, use, 2)


def two_halo_kernel(
    tiles, count, pack, left, right, own, mix, readout, wide_ext, radial_wide, total_own,
    energy_out, adjoint_out, weighted, back_left, back_right,
    halo, kernel_a, kernel_b, total, grad, order,
):
    clusters = own.shape[0]
    margin = left.shape[0]
    bases, channels, size = radial_wide.shape
    for s in range(margin):
        halo[s] = left[s]
        halo[margin + s] = right[s]
    total[...] = jnp.zeros_like(total)
    grad[...] = jnp.zeros_like(grad)
    number = select(
        tiles, count, order,
        lambda h: jnp.logical_or(h < margin, h >= margin + clusters),
    )
    layer_two_tiles(
        tiles, order, number, margin, wide_ext, pack,
        lambda h: halo[halo_slot(h, margin, clusters)],
        radial_wide, (kernel_a, kernel_b), total,
    )
    readout_wide = readout[...].astype(f32)
    for g in range(clusters):
        parts = [own[g, m * size : (m + 1) * size, :].astype(f32) for m in range(4)]
        act = dot(jnp.transpose(total[g] + total_own[g]).astype(bf16), mix[...])
        act = act + parts[0] + (parts[1] * parts[1] + parts[2] * parts[2] + parts[3] * parts[3])
        sig = 1.0 / (1.0 + jnp.exp(-act))
        energy_out[g : g + 1, :] = jnp.sum(
            jnp.transpose(act * sig * readout_wide), axis=0, keepdims=True
        )
        adjoint = readout_wide * sig * (1.0 + act * (1.0 - sig))
        adjoint_out[g] = adjoint
        high, low = split(adjoint)
        second = dot(mix[...], high, contract_cols) + dot(mix[...], low, contract_cols)
        for k in range(bases):
            weighted[g, k] = (second * radial_wide[k]).astype(bf16)

    back_tiles(
        tiles, order, number, margin, wide_ext, pack, weighted, (kernel_a, kernel_b), grad,
        lambda h: halo_slot(h, margin, clusters),
    )
    for s in range(margin):
        back_left[s] = grad[s].astype(bf16)
        back_right[s] = grad[margin + s].astype(bf16)


def two_back_kernel(
    tiles, count, pack, left, right, own, mix, adjoint, weighted, wide_ext, energy,
    first_out, feature_out, energy_out,
    kernel_a, kernel_b, grad, direct, order, sem,
):
    copy = pltpu.make_async_copy(energy, energy_out, sem)
    copy.start()
    clusters = own.shape[0]
    margin = left.shape[0]
    bases, channels, size = weighted.shape[1:]
    grad[...] = jnp.zeros_like(grad)
    for s in range(margin):
        feature_out[s] = left[s]
        feature_out[margin + clusters + s] = right[s]
    for g in range(clusters):
        feature_out[margin + g] = own[g]
    number = select(
        tiles, count, order,
        lambda h: jnp.logical_and(h >= margin, h < margin + clusters),
    )
    back_tiles(
        tiles, order, number, margin, wide_ext, pack, weighted, (kernel_a, kernel_b), grad,
        lambda h: jnp.clip(h - margin, 0, clusters - 1),
    )
    for g in range(clusters):
        direct[:size, :] = adjoint[g]
        for m in range(1, 4):
            direct[m * size : (m + 1) * size, :] = (
                2.0 * own[g, m * size : (m + 1) * size, :].astype(f32) * adjoint[g]
            )
        high, low = split(direct[...])
        first = dot(mix[...], high, contract_cols) + dot(mix[...], low, contract_cols)
        high, low = split(grad[g])
        first_out[g] = first + (dot(mix[...], high) + dot(mix[...], low))
    copy.wait()


def force_kernel(
    tiles, count, border, pack, embedded, feature, first_own, from_left, from_right,
    radial_wide, mix, weighted_two, wide_ext,
    force_out, back_left, back_right,
    first, weighted_one, product_a, product_b, center_sum, partner_sum, returned, order,
):
    clusters = first_own.shape[0]
    margin = from_left.shape[0]
    bases, channels, size = radial_wide.shape
    extent = clusters + 2 * margin
    ratios = steps_of(bases)
    for s in range(margin):
        returned[s] = dot(mix[...], from_left[s])
        returned[margin + s] = dot(mix[...], from_right[s])
    for g in range(clusters):
        first[g] = first_own[g]
    for s in range(2 * margin):
        first[border[s]] += returned[s]
    for start in range(0, channels, FINE):
        span = slice(start, start + FINE)
        scales = [radial_wide[k, span, :] for k in range(bases)]
        for g in range(clusters):
            for m in range(4):
                part = first[g, span, m * size : (m + 1) * size]
                for k in range(bases):
                    weighted_one[g, m, k, span, :] = (part * scales[k]).astype(bf16)
    center_sum[...] = jnp.zeros_like(center_sum)
    partner_sum[...] = jnp.zeros_like(partner_sum)
    number = select(tiles, count, order, lambda h: h >= 0)
    products = (product_a, product_b)

    def multiply(i, slot):
        g, h, _, _ = tile_of(tiles, order, number, i, margin)
        base = embedded[h]
        for m in range(4):
            given = jnp.concatenate([base, feature[h, m * size : (m + 1) * size, :]], axis=1)
            for k in range(0, bases, 2):
                pair = dot(
                    given,
                    jnp.concatenate(
                        [
                            jnp.concatenate([weighted_one[g, m, k], weighted_one[g, m, k + 1]], axis=1),
                            jnp.concatenate([weighted_two[g, k], weighted_two[g, k + 1]], axis=1),
                        ],
                        axis=0,
                    ),
                )
                products[slot][m, k] = pair[:, :size]
                products[slot][m, k + 1] = pair[:, size:]
                yield True

    def gather(i, slot):
        g, h, shift, key = tile_of(tiles, order, number, i, margin)
        product = products[slot]
        row = pack[g + margin]
        rows = [row[e : e + 1, :] for e in range(3)]
        sums = [None] * 3
        for start in range(0, size, FINE):
            cols = [wide_ext[h, e, start : start + FINE, :] for e in range(3)]
            offset, inverse, shifted, fall, fall_masked, gauss, ratio = pair_geometry(
                cols, rows, True, shift, key, start
            )
            unit = [part * inverse for part in offset]
            basis = [gauss * fall_masked]
            for k in range(1, bases):
                basis.append(basis[-1] * (ratio * ratios[k - 1]))
            plain, slope = [], []
            for m in range(4):
                tail = None
                weigh = None
                for k in range(bases - 1, -1, -1):
                    term = basis[k] * product[m, k, start : start + FINE, :]
                    tail = term if tail is None else tail + term
                    if k:
                        weigh = tail if weigh is None else weigh + tail
                plain.append(tail)
                slope.append(weigh)
            scale0 = shifted * fall * (-2.0 / (spread * spread)) - (shifted + first_center) * (
                4.0 / (cutoff * cutoff)
            )
            scale1 = fall * (2.0 * center_step / (spread * spread))
            bent = unit[0] * plain[1] + unit[1] * plain[2] + unit[2] * plain[3]
            slope_sum = slope[0] + unit[0] * slope[1] + unit[1] * slope[2] + unit[2] * slope[3]
            near = fall * inverse
            along = scale0 * (plain[0] + bent) + scale1 * slope_sum - near * bent
            lanes = lax.broadcasted_iota(jnp.int32, (FINE, size), 1)
            column = None
            for e in range(3):
                move = unit[e] * along + near * plain[e + 1]
                line = jnp.sum(move, axis=1, keepdims=True)
                column = line if column is None else jnp.where(lanes == e, line, column)
                part = move[:8]
                for r in range(8, FINE, 8):
                    part = part + move[r : r + 8]
                sums[e] = part if sums[e] is None else sums[e] + part
            partner_sum[h, start : start + FINE, :] += column
            if start + FINE == size:
                for e in range(3):
                    center_sum[g, e] += sums[e]
            yield True

    pipelined(number, multiply, 2 * bases, gather, size // FINE, unroll=FORCE_UNROLL, tail=False)
    lines = [jnp.transpose(partner_sum[h]) for h in range(extent)]
    for g in range(clusters):
        for e in range(3):
            force_out[e, g : g + 1, :] = (
                jnp.sum(center_sum[g, e], axis=0, keepdims=True) - lines[g + margin][e : e + 1]
            )
    for s in range(margin):
        back_left[s] = -lines[s][:ROWS]
        back_right[s] = -lines[margin + clusters + s][:ROWS]


def finish_kernel(border, own, from_left, from_right, out):
    out[...] = own[...]
    for ref, side in ((from_left, 0), (from_right, 1)):
        for s in range(ref.shape[0]):
            place = pl.ds(border[side * ref.shape[0] + s], 1)
            for e in range(3):
                out[e, place, :] += ref[s, e : e + 1, :]


smem = pl.BlockSpec(memory_space=pltpu.SMEM)
vmem = pl.BlockSpec(memory_space=pltpu.VMEM)


hbm = pl.BlockSpec(memory_space=pltpu.HBM)


def call(body, name, ins, outs, scratch, mib, cost_us=1, last_out=0, flags=None):
    return pl.pallas_call(
        body,
        name=name,
        out_shape=outs,
        in_specs=ins,
        out_specs=[vmem] * (len(outs) - last_out) + [hbm] * last_out,
        scratch_shapes=scratch,
        cost_estimate=pl.CostEstimate(
            flops=int(cost_us * 900e6), bytes_accessed=1 << 16, transcendentals=0
        ),
        compiler_params=pltpu.CompilerParams(vmem_limit_bytes=mib * 1024 * 1024, flags=flags),
    )


def swap(to_left, to_right, axis):
    count = lax.axis_size(axis)
    from_left = lax.ppermute(to_right, axis, [(i, (i + 1) % count) for i in range(count)])
    from_right = lax.ppermute(to_left, axis, [((i + 1) % count, i) for i in range(count)])
    return from_left, from_right


def shards(
    positions, species, element_embed, radial_one, mix_one, radial_two, mix_two, readout,
    tile_list, tile_count, border,
):
    clusters, _, size = positions.shape
    channels = element_embed.shape[1]
    bases = radial_one.shape[0]
    margin = border.shape[1]
    extent = clusters + 2 * margin
    slots = tile_list.shape[0]
    sds = jax.ShapeDtypeStruct
    buffer = pltpu.VMEM
    order = pltpu.SMEM((slots + 1,), jnp.int32)
    pair = [buffer((bases, 4 * size, size), bf16)] * 2
    table = jnp.concatenate([tile_list.T.reshape(-1), tile_count, border.reshape(-1)])

    def with_table(body, bordered):
        def wrapped(ref, *refs):
            views = [View(ref, 0, 2 * slots), View(ref, 2 * slots, 1)]
            if bordered:
                views.append(View(ref, 2 * slots + 1, 2 * margin))
            return body(*views, *refs)

        return wrapped

    wide = -(-element_embed.shape[0] // 128) * 128
    embed = jnp.pad(element_embed, ((0, wide - element_embed.shape[0]), (0, 0)))

    positions = positions.transpose(1, 0, 2)
    to_left, to_right = call(
        pack_kernel, "pack", [smem, vmem, vmem], [sds((margin, ROWS, size), f32)] * 2, [], 62
    )(border, positions, species)
    pack_left, pack_right = swap(to_left, to_right, "bx")
    weights = [buffer((clusters, bases * size, channels), bf16)] * 2
    own, embedded_own, wide_own, total_own = call(
        with_table(lambda *refs: one_own_kernel(*refs, margin=margin), False), "one_own", [smem] + [vmem] * 4,
        [
            sds((clusters, ROWS, size), f32),
            sds((clusters, size, channels), bf16),
            sds((clusters, 3, size, size), f32),
            sds((clusters, 4 * size, channels), f32),
        ],
        weights + pair + [order], 12, 4,
    )(table, positions, species, embed, radial_one)
    feature, to_left, to_right, pack_ext, embedded = call(
        with_table(one_halo_kernel, True), "one_halo", [smem] + [vmem] * 9,
        [
            sds((clusters, 4 * size, channels), bf16),
            sds((margin, 4 * size, channels), bf16),
            sds((margin, 4 * size, channels), bf16),
            sds((extent, ROWS, size), f32),
            sds((extent, size, channels), bf16),
        ],
        [buffer((2 * margin, bases * size, channels), bf16)] * 2
        + [buffer((2 * margin, ROWS, size), f32)]
        + pair
        + [buffer((clusters, 4 * size, channels), f32), order], 14, 4,
    )(
        table, pack_left, pack_right, own, embed, radial_one, mix_one,
        embedded_own, wide_own, total_own,
    )
    feature_left, feature_right = swap(to_left, to_right, "bx")
    total_two, wide_ext, radial_one_wide, radial_two_wide, descriptors = call(
        with_table(two_own_kernel, False), "two_own", [smem] + [vmem] * 4,
        [
            sds((clusters, channels, size), f32),
            sds((extent, 3, size, size), f32),
            sds((bases, channels, size), f32),
            sds((bases, channels, size), f32),
            sds((clusters, 4 * size, channels), bf16),
        ],
        pair + [order, pltpu.SemaphoreType.DMA], 10, 4, 1,
    )(table, pack_ext, feature, radial_one, radial_two)
    energy, adjoint, weighted_two, back_left, back_right = call(
        with_table(two_halo_kernel, False), "two_halo", [smem] + [vmem] * 9,
        [
            sds((clusters, size), f32),
            sds((clusters, size, channels), f32),
            sds((clusters, bases, channels, size), bf16),
            sds((margin, channels, 4 * size), bf16),
            sds((margin, channels, 4 * size), bf16),
        ],
        [buffer((2 * margin, 4 * size, channels), bf16)]
        + pair
        + [
            buffer((clusters, channels, size), f32),
            buffer((2 * margin, channels, 4 * size), f32),
            order,
        ], 14, 4,
    )(
        table, pack_ext, feature_left, feature_right, feature, mix_two,
        readout.reshape(1, channels), wide_ext, radial_two_wide, total_two,
    )
    grad_left, grad_right = swap(back_left, back_right, "bx")
    first, feature_ext, atom_energy = call(
        with_table(two_back_kernel, False), "two_back", [smem] + [vmem] * 9,
        [
            sds((clusters, channels, 4 * size), f32),
            sds((extent, 4 * size, channels), bf16),
            sds((clusters, size), f32),
        ],
        pair
        + [
            buffer((clusters, channels, 4 * size), f32),
            buffer((4 * size, channels), f32),
            order,
            pltpu.SemaphoreType.DMA,
        ], 12, 4, 1,
    )(
        table, pack_ext, feature_left, feature_right, feature, mix_one, adjoint,
        weighted_two, wide_ext, energy,
    )
    force, move_left, move_right = call(
        with_table(force_kernel, True), "forces", [smem] + [vmem] * 10,
        [
            sds((3, clusters, size), f32),
            sds((margin, ROWS, size), f32),
            sds((margin, ROWS, size), f32),
        ],
        [
            buffer((clusters, channels, 4 * size), f32),
            buffer((clusters, 4, bases, channels, size), bf16),
            buffer((4, bases, size, size), f32),
            buffer((4, bases, size, size), f32),
            buffer((clusters, 3, 8, size), f32),
            buffer((extent, size, size), f32),
            buffer((2 * margin, channels, 4 * size), f32),
            order,
        ], 20, 4,
    )(
        table, pack_ext, embedded, feature_ext, first, grad_left, grad_right,
        radial_one_wide, mix_one, weighted_two, wide_ext,
    )
    moved_left, moved_right = swap(move_left, move_right, "bx")
    forces = call(lambda ref, *refs: finish_kernel(View(ref, 2 * slots + 1, 2 * margin), *refs), "finish", [smem] + [vmem] * 3, [sds((3, clusters, size), f32)], [], 4)(
        table, force, moved_left, moved_right
    )[0]
    return (
        atom_energy,
        forces.transpose(1, 0, 2),
        descriptors.reshape(clusters, 4, size, channels),
    )


def solution(mesh):
    placed = (
        P(("rep", "bx"), None, None),
        P(("rep", "bx"), None),
        P(),
        P(),
        P(),
        P(),
        P(),
        P(),
        P(("rep", "bx"), None),
        P(("rep", "bx")),
        P(("rep", "bx"), None),
    )
    return jax.shard_map(
        shards,
        mesh=mesh,
        in_specs=placed,
        out_specs=(
            P(("rep", "bx"), None),
            P(("rep", "bx"), None, None),
            P(("rep", "bx"), None, None, None),
        ),
        check_vma=False,
    )
```

```python
import math

import jax
import jax.numpy as jnp
from jax import lax
from jax.experimental import pallas as pl
from jax.experimental.pallas import tpu as pltpu
from jax.sharding import PartitionSpec as P

soften = 0.25
cutoff = 3.6
spread = 0.9
first_center = 0.25
center_step = 0.45
message_scale = 0.125
dead_shift = 60.0
f32 = jnp.float32
bf16 = jnp.bfloat16
STEP = 32
FINE = 16
FORCE_UNROLL = 4
ROWS = 8

contract_cols = (((1,), (1,)), ((), ()))
contract_rows = (((0,), (0,)), ((), ()))


def dot(left, right, dims=(((1,), (0,)), ((), ()))):
    return lax.dot_general(left, right, dims, preferred_element_type=f32)


def split(value):
    high = value.astype(bf16)
    return high, (value - high.astype(f32)).astype(bf16)


def wide_columns(pack, out_ref, at):
    size = pack.shape[-1]
    for e in range(3):
        out_ref[at, e] = jnp.transpose(jnp.broadcast_to(pack[e : e + 1, :], (size, size)))


def wide_radial(radial, out_ref):
    bases, channels = radial.shape
    for k in range(bases):
        out_ref[k] = jnp.transpose(
            jnp.broadcast_to(radial[k : k + 1, :] * message_scale, (channels, channels))
        )


def pair_geometry(cols, rows, partner_rows, shift, key, start):
    if partner_rows:
        offset = [col - row for row, col in zip(rows, cols)]
    else:
        offset = [row - col for row, col in zip(rows, cols)]
    square = offset[0] * offset[0] + offset[1] * offset[1] + (offset[2] * offset[2] + shift)
    inverse = lax.rsqrt(square)
    shifted = square * inverse - first_center
    fall = jnp.maximum(1.0 - square * (1.0 / (cutoff * cutoff)), 0.0)
    shape = cols[0].shape
    apart = lax.broadcasted_iota(jnp.int32, shape, 1) - lax.broadcasted_iota(jnp.int32, shape, 0)
    fall_masked = jnp.where(apart == key + start, 0.0, fall)
    scale = math.log2(math.e) / (spread * spread)
    gauss = jnp.exp2(shifted * shifted * -scale)
    ratio = jnp.exp2(shifted * (2.0 * center_step * scale))
    return offset, inverse, shifted, fall, fall_masked, gauss, ratio


def steps_of(bases):
    base = (center_step / spread) ** 2
    return [math.exp(-base * (2 * k - 1)) for k in range(1, bases)]


class View:
    def __init__(self, ref, start, length):
        self.ref, self.start, self.shape = ref, start, (length,)

    def __getitem__(self, at):
        return self.ref[self.start + at]


def select(tiles, count, order, keep):
    number = jnp.int32(0)
    slots = tiles.shape[0] // 2
    for t in range(slots):
        order[number] = t
        wanted = jnp.logical_and(t < count[0], keep(tiles[slots + t]))
        number = number + wanted.astype(jnp.int32)
    return number


def tile_of(tiles, order, number, i, margin):
    t = order[jnp.maximum(jnp.minimum(i, number - 1), 0)]
    g, h = tiles[t], tiles[tiles.shape[0] // 2 + t]
    key = jnp.where(h == g + margin, 0, 1 << 20).astype(jnp.int32)
    shift = jnp.where(i < number, soften, soften + dead_shift).astype(f32)
    return g, h, shift, key


def weave(*streams):
    pieces = []
    for place, (count, stream) in enumerate(streams):
        pieces += [((i + 0.5) / count, place, stream) for i in range(count)]
    for _, _, stream in sorted(pieces, key=lambda piece: piece[:2]):
        next(stream)
    for _, stream in streams:
        assert next(stream, None) is None


def pipelined(number, first, first_pieces, second, second_pieces, unroll=2, tail=True):
    def step(i, carry):
        for j in range(unroll):
            at = unroll * i + j
            weave(
                (second_pieces, second(at, j % 2)),
                (first_pieces, first(at + 1, (j + 1) % 2)),
            )
        return carry

    @pl.when(number > 0)
    def _():
        weave((first_pieces, first(0, 0)))
        if not tail:
            lax.fori_loop(0, (number + unroll - 1) // unroll, step, 0)
            return
        assert unroll == 2
        lax.fori_loop(0, number // 2, step, 0)

        @pl.when(number % 2 == 1)
        def _():
            weave((second_pieces, second(number - 1, 0)))


def write_kernel(out, wide, row, partner_rows, shift, key, bases):
    size = row.shape[-1]
    ratios = steps_of(bases)
    rows = [row[e : e + 1, :] for e in range(3)]
    for start in range(0, size, STEP):
        cols = [wide(e, start, STEP) for e in range(3)]
        offset, inverse, _, fall, fall_masked, gauss, ratio = pair_geometry(
            cols, rows, partner_rows, shift, key, start
        )
        unit = [part * inverse for part in offset]
        basis = gauss * fall * fall_masked
        for k in range(bases):
            if k:
                basis = basis * (ratio * ratios[k - 1])
            for m in range(4):
                value = (basis if m == 0 else basis * unit[m - 1]).astype(bf16)
                out[k, m * size + start : m * size + start + STEP, :] = value
        yield True


def reader(ref, at):
    return lambda e, start, step: ref[at, e, start : start + step, :]


def fill_pack(out, at, positions, species, g):
    out[at] = jnp.zeros(out.shape[1:], f32)
    for e in range(3):
        out[at, e : e + 1, :] = positions[e, pl.ds(g, 1), :]
    out[at, 3:4, :] = species[pl.ds(g, 1), :].astype(f32)


def pack_kernel(border, positions, species, left_out, right_out):
    for s in range(border.shape[1]):
        fill_pack(left_out, s, positions, species, border[0, s])
        fill_pack(right_out, s, positions, species, border[1, s])


def embed_cluster(pack, embed, radial, embedded_out, weighted, rest, at, out_at):
    size = pack.shape[-1]
    col = jnp.transpose(pack)
    onehot = (
        lax.broadcasted_iota(jnp.int32, (size, embed.shape[0]), 1).astype(f32) == col[:, 3:4]
    ).astype(bf16)
    wide = dot(onehot, embed[...])
    embedded_out[out_at] = wide.astype(bf16)
    for k in range(radial.shape[0]):
        high, low = split(wide * (message_scale * radial[k : k + 1, :]))
        weighted[at, k * size : (k + 1) * size, :] = high
        rest[at, k * size : (k + 1) * size, :] = low


def layer_one_tiles(
    tiles, order, number, margin, wide_own, row_of, weights_of, kernels, total, bases
):
    def make(i, slot):
        g, h, shift, key = tile_of(tiles, order, number, i, margin)
        yield from write_kernel(
            kernels[slot], reader(wide_own, g), row_of(h), False, shift, key, bases
        )

    def use(i, slot):
        g, h, _, _ = tile_of(tiles, order, number, i, margin)
        size = total.shape[1] // 4
        weights = jnp.concatenate(weights_of(h), axis=1)
        for m in range(4):
            rows = slice(m * size, (m + 1) * size)
            both = dot(
                jnp.concatenate([kernels[slot][k, rows] for k in range(bases)], axis=1), weights
            )
            half = both.shape[1] // 2
            total[g, rows] += both[:, :half] + both[:, half:]
            yield True

    pipelined(number, make, wide_own.shape[2] // STEP, use, 4)


def one_own_kernel(
    tiles, count, positions, species, embed, radial,
    own, embedded_out, wide_own, total,
    weighted, rest, kernel_a, kernel_b, order, *, margin,
):
    clusters = own.shape[0]
    bases = radial.shape[0]
    for g in range(clusters):
        fill_pack(own, g, positions, species, g)
        wide_columns(own[g], wide_own, g)
        embed_cluster(own[g], embed, radial, embedded_out, weighted, rest, g, g)
    total[...] = jnp.zeros_like(total)
    number = select(
        tiles, count, order,
        lambda h: jnp.logical_and(h >= margin, h < margin + clusters),
    )
    layer_one_tiles(
        tiles, order, number, margin, wide_own,
        lambda h: own[jnp.clip(h - margin, 0, clusters - 1)],
        lambda h: [ref[jnp.clip(h - margin, 0, clusters - 1)] for ref in (weighted, rest)],
        (kernel_a, kernel_b), total, bases,
    )


def halo_slot(h, margin, clusters):
    return jnp.where(h < margin, h, jnp.maximum(h - clusters, 0))


def one_halo_kernel(
    tiles, count, border, left, right, own, embed, radial, mix, embedded_own, wide_own, total_own,
    feature_out, send_left, send_right, pack_out, embedded_out,
    weighted, rest, halo, kernel_a, kernel_b, total, order,
):
    clusters, _, size = own.shape
    margin = left.shape[0]
    bases = radial.shape[0]
    for s in range(margin):
        for at, ref, out_at in ((s, left, s), (margin + s, right, margin + clusters + s)):
            pack = ref[s]
            halo[at] = pack
            pack_out[out_at] = pack
            embed_cluster(pack, embed, radial, embedded_out, weighted, rest, at, out_at)
    for g in range(clusters):
        pack_out[margin + g] = own[g]
        embedded_out[margin + g] = embedded_own[g]
    total[...] = jnp.zeros_like(total)
    number = select(
        tiles, count, order,
        lambda h: jnp.logical_or(h < margin, h >= margin + clusters),
    )
    layer_one_tiles(
        tiles, order, number, margin, wide_own,
        lambda h: halo[halo_slot(h, margin, clusters)],
        lambda h: [ref[halo_slot(h, margin, clusters)] for ref in (weighted, rest)],
        (kernel_a, kernel_b), total, bases,
    )
    for g in range(clusters):
        mixed = dot((total[g] + total_own[g]).astype(bf16), mix[...])
        for m in range(4):
            part = mixed[m * size : (m + 1) * size]
            if m == 0:
                part = part + embedded_own[g].astype(f32)
            feature_out[g, m * size : (m + 1) * size, :] = part.astype(bf16)
    for s in range(margin):
        send_left[s] = feature_out[border[s]]
        send_right[s] = feature_out[border[margin + s]]


def layer_two_tiles(
    tiles, order, number, margin, wide_ext, pack, feature_of, radial_wide, kernels, total
):
    bases = radial_wide.shape[0]
    size = pack.shape[-1]

    def make(i, slot):
        g, h, shift, key = tile_of(tiles, order, number, i, margin)
        yield from write_kernel(
            kernels[slot], reader(wide_ext, h), pack[g + margin], True, shift, key, bases
        )

    def use(i, slot):
        g, h, _, _ = tile_of(tiles, order, number, i, margin)
        channel_rows = jnp.transpose(feature_of(h))
        message = None
        for k in range(0, bases, 2):
            product = dot(
                channel_rows, jnp.concatenate([kernels[slot][k], kernels[slot][k + 1]], axis=1)
            )
            for j in range(2):
                term = product[:, j * size : (j + 1) * size] * radial_wide[k + j]
                message = term if message is None else message + term
            if k == bases - 2:
                total[g] += message
            yield True

    pipelined(number, make, size // STEP, use, bases // 2)


def two_own_kernel(
    tiles, count, pack, own, radial_one, radial_two,
    total, wide_ext, radial_one_wide, radial_two_wide, descriptors,
    kernel_a, kernel_b, order, sem,
):
    copy = pltpu.make_async_copy(own, descriptors, sem)
    copy.start()
    extent, clusters = pack.shape[0], own.shape[0]
    margin = (extent - clusters) // 2
    for h in range(extent):
        wide_columns(pack[h], wide_ext, h)
    wide_radial(radial_one, radial_one_wide)
    wide_radial(radial_two, radial_two_wide)
    total[...] = jnp.zeros_like(total)
    number = select(
        tiles, count, order,
        lambda h: jnp.logical_and(h >= margin, h < margin + clusters),
    )
    layer_two_tiles(
        tiles, order, number, margin, wide_ext, pack,
        lambda h: own[jnp.clip(h - margin, 0, clusters - 1)],
        radial_two_wide, (kernel_a, kernel_b), total,
    )
    copy.wait()


def back_tiles(
    tiles, order, number, margin, wide_ext, pack, weighted, kernels, grad, place_of
):
    bases, _, size = weighted.shape[1:]

    def make(i, slot):
        g, h, shift, key = tile_of(tiles, order, number, i, margin)
        yield from write_kernel(
            kernels[slot], reader(wide_ext, g + margin), pack[h], False, shift, key, bases
        )

    def use(i, slot):
        g, h, _, _ = tile_of(tiles, order, number, i, margin)
        given = jnp.concatenate([weighted[g, k] for k in range(bases)], axis=1)
        for m in range(0, 4, 2):
            one, two = (slice((m + j) * size, (m + j + 1) * size) for j in range(2))
            grad[place_of(h), :, m * size : (m + 2) * size] += dot(
                given,
                jnp.concatenate(
                    [
                        jnp.concatenate([kernels[slot][k, one], kernels[slot][k, two]], axis=1)
                        for k in range(bases)
                    ],
                    axis=0,
                ),
            )
            yield True

    pipelined(number, make, size // STEP, use, 2)


def two_halo_kernel(
    tiles, count, pack, left, right, own, mix, readout, wide_ext, radial_wide, total_own,
    energy_out, adjoint_out, weighted, back_left, back_right,
    halo, kernel_a, kernel_b, total, grad, order,
):
    clusters = own.shape[0]
    margin = left.shape[0]
    bases, channels, size = radial_wide.shape
    for s in range(margin):
        halo[s] = left[s]
        halo[margin + s] = right[s]
    total[...] = jnp.zeros_like(total)
    grad[...] = jnp.zeros_like(grad)
    number = select(
        tiles, count, order,
        lambda h: jnp.logical_or(h < margin, h >= margin + clusters),
    )
    layer_two_tiles(
        tiles, order, number, margin, wide_ext, pack,
        lambda h: halo[halo_slot(h, margin, clusters)],
        radial_wide, (kernel_a, kernel_b), total,
    )
    readout_wide = readout[...].astype(f32)
    for g in range(clusters):
        parts = [own[g, m * size : (m + 1) * size, :].astype(f32) for m in range(4)]
        act = dot(jnp.transpose(total[g] + total_own[g]).astype(bf16), mix[...])
        act = act + parts[0] + (parts[1] * parts[1] + parts[2] * parts[2] + parts[3] * parts[3])
        sig = 1.0 / (1.0 + jnp.exp(-act))
        energy_out[g : g + 1, :] = jnp.sum(
            jnp.transpose(act * sig * readout_wide), axis=0, keepdims=True
        )
        adjoint = readout_wide * sig * (1.0 + act * (1.0 - sig))
        adjoint_out[g] = adjoint
        high = adjoint.astype(bf16)
        second = dot(mix[...], high, contract_cols)
        for k in range(bases):
            weighted[g, k] = (second * radial_wide[k]).astype(bf16)

    back_tiles(
        tiles, order, number, margin, wide_ext, pack, weighted, (kernel_a, kernel_b), grad,
        lambda h: halo_slot(h, margin, clusters),
    )
    for s in range(margin):
        back_left[s] = grad[s].astype(bf16)
        back_right[s] = grad[margin + s].astype(bf16)


def two_back_kernel(
    tiles, count, pack, left, right, own, mix, adjoint, weighted, wide_ext, energy,
    first_out, feature_out, energy_out,
    kernel_a, kernel_b, grad, direct, order, sem,
):
    copy = pltpu.make_async_copy(energy, energy_out, sem)
    copy.start()
    clusters = own.shape[0]
    margin = left.shape[0]
    bases, channels, size = weighted.shape[1:]
    grad[...] = jnp.zeros_like(grad)
    for s in range(margin):
        feature_out[s] = left[s]
        feature_out[margin + clusters + s] = right[s]
    for g in range(clusters):
        feature_out[margin + g] = own[g]
    number = select(
        tiles, count, order,
        lambda h: jnp.logical_and(h >= margin, h < margin + clusters),
    )
    back_tiles(
        tiles, order, number, margin, wide_ext, pack, weighted, (kernel_a, kernel_b), grad,
        lambda h: jnp.clip(h - margin, 0, clusters - 1),
    )
    for g in range(clusters):
        direct[:size, :] = adjoint[g]
        for m in range(1, 4):
            direct[m * size : (m + 1) * size, :] = (
                2.0 * own[g, m * size : (m + 1) * size, :].astype(f32) * adjoint[g]
            )
        first_out[g] = dot(mix[...], direct[...].astype(bf16), contract_cols) + dot(
            mix[...], grad[g].astype(bf16)
        )
    copy.wait()


def force_kernel(
    tiles, count, border, pack, embedded, feature, first_own, from_left, from_right,
    radial_wide, mix, weighted_two, wide_ext,
    force_out, back_left, back_right,
    first, weighted_one, product_a, product_b, center_sum, partner_sum, returned, order,
):
    clusters = first_own.shape[0]
    margin = from_left.shape[0]
    bases, channels, size = radial_wide.shape
    extent = clusters + 2 * margin
    ratios = steps_of(bases)
    for s in range(margin):
        returned[s] = dot(mix[...], from_left[s])
        returned[margin + s] = dot(mix[...], from_right[s])
    for g in range(clusters):
        first[g] = first_own[g]
    for s in range(2 * margin):
        first[border[s]] += returned[s]
    for start in range(0, channels, FINE):
        span = slice(start, start + FINE)
        scales = [radial_wide[k, span, :] for k in range(bases)]
        for g in range(clusters):
            for m in range(4):
                part = first[g, span, m * size : (m + 1) * size]
                for k in range(bases):
                    weighted_one[g, m, k, span, :] = (part * scales[k]).astype(bf16)
    center_sum[...] = jnp.zeros_like(center_sum)
    partner_sum[...] = jnp.zeros_like(partner_sum)
    number = select(tiles, count, order, lambda h: h >= 0)
    products = (product_a, product_b)

    def multiply(i, slot):
        g, h, _, _ = tile_of(tiles, order, number, i, margin)
        base = embedded[h]
        for m in range(4):
            given = jnp.concatenate([base, feature[h, m * size : (m + 1) * size, :]], axis=1)
            for k in range(0, bases, 2):
                pair = dot(
                    given,
                    jnp.concatenate(
                        [
                            jnp.concatenate([weighted_one[g, m, k], weighted_one[g, m, k + 1]], axis=1),
                            jnp.concatenate([weighted_two[g, k], weighted_two[g, k + 1]], axis=1),
                        ],
                        axis=0,
                    ),
                )
                products[slot][m, k] = pair[:, :size]
                products[slot][m, k + 1] = pair[:, size:]
                yield True

    def gather(i, slot):
        g, h, shift, key = tile_of(tiles, order, number, i, margin)
        product = products[slot]
        row = pack[g + margin]
        rows = [row[e : e + 1, :] for e in range(3)]
        sums = [None] * 3
        for start in range(0, size, FINE):
            cols = [wide_ext[h, e, start : start + FINE, :] for e in range(3)]
            offset, inverse, shifted, fall, fall_masked, gauss, ratio = pair_geometry(
                cols, rows, True, shift, key, start
            )
            unit = [part * inverse for part in offset]
            basis = [gauss * fall_masked]
            for k in range(1, bases):
                basis.append(basis[-1] * (ratio * ratios[k - 1]))
            plain, slope = [], []
            for m in range(4):
                tail = None
                weigh = None
                for k in range(bases - 1, -1, -1):
                    term = basis[k] * product[m, k, start : start + FINE, :]
                    tail = term if tail is None else tail + term
                    if k:
                        weigh = tail if weigh is None else weigh + tail
                plain.append(tail)
                slope.append(weigh)
            scale0 = shifted * fall * (-2.0 / (spread * spread)) - (shifted + first_center) * (
                4.0 / (cutoff * cutoff)
            )
            scale1 = fall * (2.0 * center_step / (spread * spread))
            bent = unit[0] * plain[1] + unit[1] * plain[2] + unit[2] * plain[3]
            slope_sum = slope[0] + unit[0] * slope[1] + unit[1] * slope[2] + unit[2] * slope[3]
            near = fall * inverse
            along = scale0 * (plain[0] + bent) + scale1 * slope_sum - near * bent
            lanes = lax.broadcasted_iota(jnp.int32, (FINE, size), 1)
            column = None
            for e in range(3):
                move = unit[e] * along + near * plain[e + 1]
                line = jnp.sum(move, axis=1, keepdims=True)
                column = line if column is None else jnp.where(lanes == e, line, column)
                part = move[:8]
                for r in range(8, FINE, 8):
                    part = part + move[r : r + 8]
                sums[e] = part if sums[e] is None else sums[e] + part
            partner_sum[h, start : start + FINE, :] += column
            if start + FINE == size:
                for e in range(3):
                    center_sum[g, e] += sums[e]
            yield True

    pipelined(number, multiply, 2 * bases, gather, size // FINE, unroll=FORCE_UNROLL, tail=False)
    lines = [jnp.transpose(partner_sum[h]) for h in range(extent)]
    for g in range(clusters):
        for e in range(3):
            force_out[e, g : g + 1, :] = (
                jnp.sum(center_sum[g, e], axis=0, keepdims=True) - lines[g + margin][e : e + 1]
            )
    for s in range(margin):
        back_left[s] = -lines[s][:ROWS]
        back_right[s] = -lines[margin + clusters + s][:ROWS]


def finish_kernel(border, own, from_left, from_right, out):
    out[...] = own[...]
    for ref, side in ((from_left, 0), (from_right, 1)):
        for s in range(ref.shape[0]):
            place = pl.ds(border[side * ref.shape[0] + s], 1)
            for e in range(3):
                out[e, place, :] += ref[s, e : e + 1, :]


smem = pl.BlockSpec(memory_space=pltpu.SMEM)
vmem = pl.BlockSpec(memory_space=pltpu.VMEM)


hbm = pl.BlockSpec(memory_space=pltpu.HBM)


def call(body, name, ins, outs, scratch, mib, cost_us=1, last_out=0, flags=None):
    return pl.pallas_call(
        body,
        name=name,
        out_shape=outs,
        in_specs=ins,
        out_specs=[vmem] * (len(outs) - last_out) + [hbm] * last_out,
        scratch_shapes=scratch,
        cost_estimate=pl.CostEstimate(
            flops=int(cost_us * 900e6), bytes_accessed=1 << 16, transcendentals=0
        ),
        compiler_params=pltpu.CompilerParams(vmem_limit_bytes=mib * 1024 * 1024, flags=flags),
    )


def swap(to_left, to_right, axis):
    count = lax.axis_size(axis)
    from_left = lax.ppermute(to_right, axis, [(i, (i + 1) % count) for i in range(count)])
    from_right = lax.ppermute(to_left, axis, [((i + 1) % count, i) for i in range(count)])
    return from_left, from_right


def shards(
    positions, species, element_embed, radial_one, mix_one, radial_two, mix_two, readout,
    tile_list, tile_count, border,
):
    clusters, _, size = positions.shape
    channels = element_embed.shape[1]
    bases = radial_one.shape[0]
    margin = border.shape[1]
    extent = clusters + 2 * margin
    slots = tile_list.shape[0]
    sds = jax.ShapeDtypeStruct
    buffer = pltpu.VMEM
    order = pltpu.SMEM((slots + 1,), jnp.int32)
    pair = [buffer((bases, 4 * size, size), bf16)] * 2
    table = jnp.concatenate([tile_list.T.reshape(-1), tile_count, border.reshape(-1)])

    def with_table(body, bordered):
        def wrapped(ref, *refs):
            views = [View(ref, 0, 2 * slots), View(ref, 2 * slots, 1)]
            if bordered:
                views.append(View(ref, 2 * slots + 1, 2 * margin))
            return body(*views, *refs)

        return wrapped

    wide = -(-element_embed.shape[0] // 128) * 128
    embed = jnp.pad(element_embed, ((0, wide - element_embed.shape[0]), (0, 0)))

    positions = positions.transpose(1, 0, 2)
    to_left, to_right = call(
        pack_kernel, "pack", [smem, vmem, vmem], [sds((margin, ROWS, size), f32)] * 2, [], 62
    )(border, positions, species)
    pack_left, pack_right = swap(to_left, to_right, "bx")
    weights = [buffer((clusters, bases * size, channels), bf16)] * 2
    own, embedded_own, wide_own, total_own = call(
        with_table(lambda *refs: one_own_kernel(*refs, margin=margin), False), "one_own", [smem] + [vmem] * 4,
        [
            sds((clusters, ROWS, size), f32),
            sds((clusters, size, channels), bf16),
            sds((clusters, 3, size, size), f32),
            sds((clusters, 4 * size, channels), f32),
        ],
        weights + pair + [order], 12, 4,
    )(table, positions, species, embed, radial_one)
    feature, to_left, to_right, pack_ext, embedded = call(
        with_table(one_halo_kernel, True), "one_halo", [smem] + [vmem] * 9,
        [
            sds((clusters, 4 * size, channels), bf16),
            sds((margin, 4 * size, channels), bf16),
            sds((margin, 4 * size, channels), bf16),
            sds((extent, ROWS, size), f32),
            sds((extent, size, channels), bf16),
        ],
        [buffer((2 * margin, bases * size, channels), bf16)] * 2
        + [buffer((2 * margin, ROWS, size), f32)]
        + pair
        + [buffer((clusters, 4 * size, channels), f32), order], 14, 4,
    )(
        table, pack_left, pack_right, own, embed, radial_one, mix_one,
        embedded_own, wide_own, total_own,
    )
    feature_left, feature_right = swap(to_left, to_right, "bx")
    total_two, wide_ext, radial_one_wide, radial_two_wide, descriptors = call(
        with_table(two_own_kernel, False), "two_own", [smem] + [vmem] * 4,
        [
            sds((clusters, channels, size), f32),
            sds((extent, 3, size, size), f32),
            sds((bases, channels, size), f32),
            sds((bases, channels, size), f32),
            sds((clusters, 4 * size, channels), bf16),
        ],
        pair + [order, pltpu.SemaphoreType.DMA], 10, 4, 1,
    )(table, pack_ext, feature, radial_one, radial_two)
    energy, adjoint, weighted_two, back_left, back_right = call(
        with_table(two_halo_kernel, False), "two_halo", [smem] + [vmem] * 9,
        [
            sds((clusters, size), f32),
            sds((clusters, size, channels), f32),
            sds((clusters, bases, channels, size), bf16),
            sds((margin, channels, 4 * size), bf16),
            sds((margin, channels, 4 * size), bf16),
        ],
        [buffer((2 * margin, 4 * size, channels), bf16)]
        + pair
        + [
            buffer((clusters, channels, size), f32),
            buffer((2 * margin, channels, 4 * size), f32),
            order,
        ], 14, 4,
    )(
        table, pack_ext, feature_left, feature_right, feature, mix_two,
        readout.reshape(1, channels), wide_ext, radial_two_wide, total_two,
    )
    grad_left, grad_right = swap(back_left, back_right, "bx")
    first, feature_ext, atom_energy = call(
        with_table(two_back_kernel, False), "two_back", [smem] + [vmem] * 9,
        [
            sds((clusters, channels, 4 * size), f32),
            sds((extent, 4 * size, channels), bf16),
            sds((clusters, size), f32),
        ],
        pair
        + [
            buffer((clusters, channels, 4 * size), f32),
            buffer((4 * size, channels), f32),
            order,
            pltpu.SemaphoreType.DMA,
        ], 12, 4, 1,
    )(
        table, pack_ext, feature_left, feature_right, feature, mix_one, adjoint,
        weighted_two, wide_ext, energy,
    )
    force, move_left, move_right = call(
        with_table(force_kernel, True), "forces", [smem] + [vmem] * 10,
        [
            sds((3, clusters, size), f32),
            sds((margin, ROWS, size), f32),
            sds((margin, ROWS, size), f32),
        ],
        [
            buffer((clusters, channels, 4 * size), f32),
            buffer((clusters, 4, bases, channels, size), bf16),
            buffer((4, bases, size, size), f32),
            buffer((4, bases, size, size), f32),
            buffer((clusters, 3, 8, size), f32),
            buffer((extent, size, size), f32),
            buffer((2 * margin, channels, 4 * size), f32),
            order,
        ], 20, 4,
    )(
        table, pack_ext, embedded, feature_ext, first, grad_left, grad_right,
        radial_one_wide, mix_one, weighted_two, wide_ext,
    )
    moved_left, moved_right = swap(move_left, move_right, "bx")
    forces = call(lambda ref, *refs: finish_kernel(View(ref, 2 * slots + 1, 2 * margin), *refs), "finish", [smem] + [vmem] * 3, [sds((3, clusters, size), f32)], [], 4)(
        table, force, moved_left, moved_right
    )[0]
    return (
        atom_energy,
        forces.transpose(1, 0, 2),
        descriptors.reshape(clusters, 4, size, channels),
    )


def solution(mesh):
    placed = (
        P(("rep", "bx"), None, None),
        P(("rep", "bx"), None),
        P(),
        P(),
        P(),
        P(),
        P(),
        P(),
        P(("rep", "bx"), None),
        P(("rep", "bx")),
        P(("rep", "bx"), None),
    )
    return jax.shard_map(
        shards,
        mesh=mesh,
        in_specs=placed,
        out_specs=(
            P(("rep", "bx"), None),
            P(("rep", "bx"), None, None),
            P(("rep", "bx"), None, None, None),
        ),
        check_vma=False,
    )
```
